32 devices in a mesh: sub: 32 (over z, y, x, core).
Axes of the slice: x: 2, y: 2, z: 4, core: 2. Of those that a mesh axis runs over, the one named last changes fastest.
Arguments:
- images: float32 [2, 4, 512, 4096], P(None, None, 'sub'), may hold values from -6 to 6
- anchors: int32 [128], P('sub'), may hold values from 0 to 4095, as said below
- patches: int32 [128], P('sub'), may hold values from 0 to 31
- coeffs: float32 [4, 45, 32], P(None, None, 'sub'), may hold values from -1.2 to 1.2
- zbasis: float32 [45, 4096], replicated, may hold values from -4 to 4
Outputs:
- new_coeffs: float32 [4, 45, 32], P(None, None, 'sub')
- last_gradient: float32 [4, 45, 32], P(None, None, 'sub')
The draws below stay inside these ranges and needn't reach their ends.
Inputs may be any that keep to these rules, and one draw needn't show every extreme that they name: `anchors`: the first column of subfield s lies among the 128 columns that begin at 128 * (s // 4).
All inputs are finite; a program needn't handle non-finite values.
Results may differ from the reference program's by a relative error of at most 0.0003.
Values sent between devices are 32-bit elements; how exact they have to be, the bound alone decides.
A program may use at most 128 MiB of HBM per device.

```python
import math
import jax
import jax.numpy as jnp
import numpy as np
from jax import lax

SUB = 128
W = 4096
MODES = 45
CH = 2
FRAMES = 4
TR = 4
ITERS = 2
PUP = 64
H = 512
SUBS = 128
NP = 32


def draw_anchors(key, part):
    strip_width = W // (SUBS // TR)
    offsets = jax.random.randint(key, (SUBS,), 0, strip_width, dtype=jnp.int32)
    offsets = offsets.at[0].set(0).at[SUBS - 1].set(strip_width - 1)
    column_strips = jnp.arange(SUBS, dtype=jnp.int32) // TR
    return (column_strips * strip_width + offsets).astype(jnp.int32)


def set_ends(array, key, low, largest):
    longest = array.shape.index(max(array.shape))
    spots = []
    for shift in (0, 1):
        where = [jax.random.randint(jax.random.fold_in(key, axis), (), 0, length) for axis, length in enumerate(array.shape)]
        where[longest] = (where[longest] + shift) % array.shape[longest]
        spots.append(tuple(where))
    return array.at[spots[0]].set(low).at[spots[1]].set(largest)


def shard_levels(own_key, shape, shards, low, largest):
    level = 1.0
    for axis_at, parts in shards:
        steps = jax.random.uniform(jax.random.fold_in(jax.random.fold_in(own_key, 6), axis_at), (parts,), jnp.float32, low / len(shards), largest / len(shards))
        level = level * jnp.repeat(jnp.exp(steps), shape[axis_at] // parts).reshape((-1,) + (1,) * (len(shape) - 1 - axis_at))
    return level


def rank_bounds(number_of, lean):
    portions = [(1 << 20) // math.isqrt(rank ** lean) + 1 for rank in range(1, number_of + 1)]
    deviation = 1 + sum(portions) // (1 << 30)
    return np.cumsum(np.array([max(1, weight // deviation) for weight in portions]))


def ranked(own_key, dims, number_of, lean):
    grid = rank_bounds(number_of, lean)
    pick = jax.random.randint(jax.random.fold_in(own_key, 1), dims, 0, int(grid[number_of - 1]))
    grade = jnp.searchsorted(jnp.asarray(grid, jnp.int32), pick, side="right")
    return jax.random.permutation(jax.random.fold_in(own_key, 2), number_of)[grade].astype(jnp.int32)


def bell_draw(key, dims, spread, reach, shards=(), kind=jnp.bfloat16):
    result = spread * jax.random.normal(key, dims, jnp.float32)
    if shards:
        result = result * shard_levels(key, dims, shards, -0.22, 0.18)
    return jnp.clip(result, -reach, reach).astype(kind)


def setup_inputs(seed: int = 0) -> dict:
    keys = jax.random.split(jax.random.key(seed), 6)
    images = bell_draw(keys[0], (CH, FRAMES, H, W), 1.0, 6.0, ((2, 32),), jnp.float32)
    anchors = draw_anchors(jax.random.fold_in(keys[5], 71), 0)
    patches = set_ends(ranked(keys[2], (SUBS,), NP, 2), jax.random.fold_in(keys[2], 3), 0, NP - 1).astype(jnp.int32)
    coeffs = bell_draw(keys[3], (FRAMES, MODES, NP), 0.2, 1.2, ((2, 32),), jnp.float32)
    zbasis = bell_draw(keys[4], (MODES, PUP * PUP), 1.0, 4.0, (), jnp.float32)
    return {"images": images, "anchors": anchors, "patches": patches, "coeffs": coeffs, "zbasis": zbasis}


GAMMA = 0.01
STEP_SIZE = 0.05

def taper(length):
    cells = jnp.arange(length, dtype=jnp.float32)
    return 0.5 - 0.5 * jnp.cos(2.0 * math.pi * (cells + 0.5) / length)

def aperture(width):
    centred = jnp.arange(width, dtype=jnp.float32) - width / 2 + 0.5
    radius = centred[:, None] ** 2 + centred[None, :] ** 2
    return (radius <= (width / 2) ** 2).astype(jnp.float32)

def reference(images, anchors, patches, coeffs, zbasis):
    window_two = taper(SUB)[:, None] * taper(SUB)[None, :]
    padded = jnp.pad(images, ((0, 0), (0, 0), (0, 0), (0, SUB)))
    pupil_mask = aperture(PUP)
    pupil_area = jnp.sum(pupil_mask)
    ratios = 1.0 / (1.0 + 0.25 * jnp.arange(CH, dtype=jnp.float32))
    zero_index = jnp.zeros((), jnp.int32)

    def subfield_loss(coefficients, which):
        row_tile = (which % TR).astype(jnp.int32)
        start_row = (row_tile * SUB).astype(jnp.int32)
        start_col = anchors[which].astype(jnp.int32)
        window_cells = lax.dynamic_slice(padded, (zero_index, zero_index, start_row, start_col), (CH, FRAMES, SUB, SUB))
        spectrum = jnp.fft.fft2(window_cells * window_two)
        chosen = lax.dynamic_index_in_dim(coefficients, patches[which].astype(jnp.int32), axis=2, keepdims=False)
        phases = jnp.dot(chosen, zbasis, precision=lax.Precision.HIGHEST).reshape(FRAMES, PUP, PUP)
        scaled = ratios[:, None, None, None] * phases[None]
        pupil = pupil_mask * jnp.exp(1j * scaled)
        field = jnp.fft.fft2(pupil, s=(SUB, SUB))
        psf_values = jnp.abs(field) ** 2 / (SUB * SUB * pupil_area)
        otf = jnp.fft.fft2(psf_values)
        power_sum = lax.optimization_barrier(jnp.sum(jnp.abs(spectrum) ** 2, axis=1))
        cross = lax.optimization_barrier(jnp.sum(spectrum * jnp.conj(otf), axis=1))
        denominator = lax.optimization_barrier(jnp.sum(jnp.abs(otf) ** 2, axis=1)) + GAMMA
        return jnp.sum(power_sum - jnp.abs(cross) ** 2 / denominator) / SUB ** 4

    def total_loss(coefficients):
        losses = lax.map(lambda which: subfield_loss(coefficients, which), jnp.arange(SUBS, dtype=jnp.int32))
        return jnp.sum(losses)
    current = coeffs
    gradient = jnp.zeros_like(coeffs)
    for iteration in range(ITERS):
        gradient = jax.grad(total_loss)(current)
        current = current - STEP_SIZE * gradient
    return (current, gradient)
```

```python
import functools
import math

import jax
import jax.numpy as jnp
import ml_dtypes
import numpy as np
from jax import lax
from jax.experimental import pallas as pl
from jax.experimental.pallas import tpu as pltpu
from jax.sharding import PartitionSpec as P

SUB = 128
CH = 2
FRAMES = 4
FIELDS = CH * FRAMES
SLOT = 64
TR = 4
ITERS = 2
PUP = 64
HALF = 72
GAMMA = 0.01
STEP_SIZE = 0.05
F32 = jnp.float32
BF16 = jnp.bfloat16
VMEM_LIMIT = 48 << 20
HIGHEST = lax.Precision.HIGHEST


def split_np(matrix):
    matrix = np.asarray(matrix, np.float32)
    high = matrix.astype(ml_dtypes.bfloat16)
    low = (matrix - high.astype(np.float32)).astype(ml_dtypes.bfloat16)
    return high, low


def make_tables():
    k = np.arange(SUB)
    angle = 2.0 * np.pi * (np.outer(k, k) % SUB) / SUB
    cos, sin = np.cos(angle), np.sin(angle)
    taper = 0.5 - 0.5 * np.cos(2.0 * np.pi * (k + 0.5) / SUB)
    right = np.zeros((2, 2, PUP, 2, 2, SUB))
    for half in range(2):
        right[0, half, :, half, 0] = cos[:PUP]
        right[0, half, :, half, 1] = -sin[:PUP]
        right[1, half, :, half, 0] = sin[:PUP]
        right[1, half, :, half, 1] = cos[:PUP]
    right = right.reshape(2 * SUB, 4 * SUB)
    left = np.block([[cos[:, :PUP], sin[:, :PUP]], [-sin[:, :PUP], cos[:, :PUP]]])
    left = left.reshape(2 * SUB, 2, PUP // 2, 2).transpose(0, 1, 3, 2).reshape(2 * SUB, SUB)
    rows_cos, rows_sin = np.zeros((HALF, SUB)), np.zeros((HALF, SUB))
    rows_cos[:65], rows_sin[:65] = cos[:65], sin[:65]
    rows = np.concatenate([rows_cos, rows_sin], 0)
    mixed = np.block([[cos, -sin], [-sin, -cos]])
    weight = np.zeros((HALF, 1))
    weight[:65] = 2.0
    weight[0] = weight[64] = 1.0
    centred = np.arange(PUP) - PUP / 2 + 0.5
    mask = (centred[:, None] ** 2 + centred[None, :] ** 2 <= (PUP / 2) ** 2).astype(np.float32)
    area = float(mask.sum())
    mask = mask.reshape(PUP // 2, SUB)
    return {
        "right": right,
        "right_t": right.T,
        "left": left,
        "left_t": left.T,
        "rows": rows,
        "rows_t": rows.T,
        "mixed": mixed,
        "data_rows": rows * taper[None, :],
        "data_mixed": np.concatenate([taper, taper])[:, None] * mixed,
        "weight": np.broadcast_to(weight, (HALF, SUB)).astype(np.float32) * np.float32(-2.0 / SUB**4),
        "mask": mask,
        "area": area,
    }


def pack_tables(tables):
    split_tables = {name: split_np(tables[name]) for name in tables if name not in ("weight", "mask", "area")}
    for half in range(2):
        split_tables["right%d" % half] = tuple(
            part[:, half * 2 * SUB : (half + 1) * 2 * SUB] for part in split_tables["right"]
        )
    del split_tables["right"]
    for name in ("left", "rows", "data_rows"):
        high, low = split_tables[name]
        split_tables[name] = (np.concatenate([high, high], 1), low)
    spots, parts, at = {}, [], 0
    for name in sorted(split_tables):
        for part in split_tables[name]:
            spots.setdefault(name, []).append((at, part.shape[0], part.shape[1]))
            parts.append(np.pad(part, ((0, 0), (0, 2 * SUB - part.shape[1]))))
            at += part.shape[0]
    return np.concatenate(parts, 0), spots


def views(ref, spots, *names):
    return [ref.at[pl.ds(at, size), pl.ds(0, width)] for name in names for at, size, width in spots[name]]


def split(value):
    high = value.astype(BF16)
    low = (value - high.astype(F32)).astype(BF16)
    return high, low


def dot(a, b):
    return jnp.dot(a, b, preferred_element_type=F32)


def const_left(high_ref, low_ref, value):
    high, low = split(value)
    table = high_ref[...]
    return dot(table, high) + (dot(table, low) + dot(low_ref[...], high))


def const_right(value, high_ref, low_ref):
    high, low = split(value)
    table = high_ref[...]
    return dot(high, table) + (dot(low, table) + dot(high, low_ref[...]))


def sin_cos(angle):
    turns = jnp.floor(angle * np.float32(2.0 / math.pi) + 0.5)
    rest = angle - turns * np.float32(1.5703125)
    rest = rest - turns * np.float32(4.8351287841796875e-4)
    rest = rest - turns * np.float32(3.1385570764541626e-7)
    rest = rest - turns * np.float32(6.0771005065061922e-11)
    square = rest * rest
    sine = rest + rest * square * (
        -1.6666654611e-1 + square * (8.3321608736e-3 + square * -1.9515295891e-4)
    )
    cosine = 1.0 - 0.5 * square + square * square * (
        4.166664568298827e-2 + square * (-1.388731625493765e-3 + square * 2.443315711809948e-5)
    )
    quadrant = turns - 4.0 * jnp.floor(turns * 0.25)
    odd = (quadrant == 1.0) | (quadrant == 3.0)
    base_sin = jnp.where(odd, cosine, sine)
    base_cos = jnp.where(odd, sine, cosine)
    out_sin = jnp.where(quadrant >= 2.0, -base_sin, base_sin)
    out_cos = jnp.where((quadrant == 1.0) | (quadrant == 2.0), -base_cos, base_cos)
    return out_sin, out_cos


def stacked_left(twice_ref, low_ref, value):
    high, low = split(value)
    return dot(twice_ref[...], jnp.concatenate([high, low], 0)) + dot(low_ref[...], high)


def half_plane(images, rows_twice, rows_low, mixed_high, mixed_low):
    columns = stacked_left(rows_twice, rows_low, images)
    stacked = jnp.concatenate(
        [
            jnp.concatenate(
                [columns[:HALF, f * SUB : (f + 1) * SUB], columns[HALF:, f * SUB : (f + 1) * SUB]], 1
            )
            for f in range(FIELDS)
        ],
        0,
    )
    return const_right(stacked, mixed_high, mixed_low)


def forward_math(scale, phase, mask_ref, tables):
    left_twice, left_low, rows_twice, rows_low, mixed_high, mixed_low = tables[4:]
    q = PUP // 2
    phase = jnp.concatenate([phase * np.float32(1.0 / (1.0 + 0.25 * c)) for c in range(CH)], 0)
    sine, cosine = sin_cos(phase)
    mask = jnp.concatenate([mask_ref[:q]] * FIELDS, 0)
    pupil = jnp.concatenate([mask * cosine, mask * sine], 1)
    half = jnp.concatenate([const_right(pupil, *tables[:2]), const_right(pupil, *tables[2:4])], 1)
    blocks = jnp.concatenate(
        [
            jnp.concatenate(
                [half[f * q : (f + 1) * q, n * SUB : (n + 1) * SUB] for n in (0, 2, 1, 3)], 0
            )
            for f in range(FIELDS)
        ],
        1,
    )
    field = stacked_left(left_twice, left_low, blocks)
    psf = (field[:SUB] * field[:SUB] + field[SUB:] * field[SUB:]) * scale
    return half_plane(psf, rows_twice, rows_low, mixed_high, mixed_low), field, pupil


def backward_math(scale, data, otf, field, pupil, weight_ref, tables):
    mixed_high, mixed_low, rows_high, rows_low, left_high, left_low, right_high, right_low = tables
    weight = weight_ref[PUP // 2 :]
    bars = []
    for c in range(CH):
        parts = []
        cross_real = cross_imag = power = None
        for f in range(c * FRAMES, (c + 1) * FRAMES):
            d, o = data[f * HALF : (f + 1) * HALF], otf[f * HALF : (f + 1) * HALF]
            dr, di, orr, oi = d[:, :SUB], d[:, SUB:], o[:, :SUB], o[:, SUB:]
            parts.append((dr, di, orr, oi))
            terms = (dr * orr + di * oi, di * orr - dr * oi, orr * orr + oi * oi)
            if cross_real is None:
                cross_real, cross_imag, power = terms
            else:
                cross_real = cross_real + terms[0]
                cross_imag = cross_imag + terms[1]
                power = power + terms[2]
        inverse = 1.0 / (power + GAMMA)
        slope = weight * inverse
        xr, xi = cross_real * inverse, cross_imag * inverse
        share = weight * (xr * xr + xi * xi)
        cross_real, cross_imag = cross_real * slope, cross_imag * slope
        for dr, di, orr, oi in parts:
            bar_real = cross_real * dr + cross_imag * di - share * orr
            bar_imag = cross_real * di - cross_imag * dr - share * oi
            bars.append(jnp.concatenate([bar_real, bar_imag], 1))
    columns = const_right(jnp.concatenate(bars, 0), mixed_high, mixed_low)
    stacked = jnp.concatenate(
        [
            jnp.concatenate(
                [columns[f * HALF : (f + 1) * HALF, :SUB], columns[f * HALF : (f + 1) * HALF, SUB:]], 0
            )
            for f in range(FIELDS)
        ],
        1,
    )
    psf_bar = const_left(rows_high, rows_low, stacked) * (2.0 * scale)
    field_bar = jnp.concatenate([field[:SUB] * psf_bar, field[SUB:] * psf_bar], 0)
    half_bar = const_left(left_high, left_low, field_bar)
    q = PUP // 2
    rows = jnp.concatenate(
        [
            jnp.concatenate(
                [half_bar[n * q : (n + 1) * q, f * SUB : (f + 1) * SUB] for n in (0, 2, 1, 3)], 1
            )
            for f in range(FIELDS)
        ],
        0,
    )
    pupil_bar = const_right(rows, right_high, right_low)
    phase_bar = pupil[:, :SUB] * pupil_bar[:, SUB:] - pupil[:, SUB:] * pupil_bar[:, :SUB]
    size = FRAMES * q
    total = phase_bar[:size]
    for c in range(1, CH):
        total = total + phase_bar[c * size : (c + 1) * size] * np.float32(1.0 / (1.0 + 0.25 * c))
    return total


FORWARD = ("right0", "right1", "left", "rows", "mixed")
BACKWARD = ("mixed", "rows_t", "left_t", "right_t")
DATA = ("data_rows", "data_mixed")
MODE_ROWS = 48
MESH = pl.DeviceIdType.MESH


def plan(n, width, rows):
    team = n // TR
    share = n * 4 // TR // team
    strip = width * TR // (n * 4)
    first = [k * strip // SUB for k in range(share)]
    return team, share, strip, first, share * strip // SUB + 1


def mega_kernel(
    scale,
    spots,
    n,
    width,
    rows,
    images_ref,
    anchors_ref,
    patches_ref,
    coeffs_ref,
    zbasis_ref,
    fixed_ref,
    pack_hbm,
    new_ref,
    grad_ref,
    tile_ref,
    everyone,
    owners,
    strips,
    pieces,
    zraw,
    zpad,
    ztable,
    pack_ref,
    phase_ref,
    total_ref,
    otf_ref,
    field_ref,
    pupil_ref,
    data_ref,
    current,
    wanted,
    mine_ref,
    slopes,
    local_sem,
    send_sem,
    recv_sem,
    strip_send,
    strip_recv,
    strip_local,
):
    me = lax.axis_index("sub")
    team, share, strip, first, count = plan(n, width, rows)
    tile = me // team
    place = lax.rem(me, team)
    barrier = pltpu.get_barrier_semaphore()

    def greet(step, carry):
        pl.semaphore_signal(barrier, inc=1, device_id=(lax.rem(me + step, n),), device_id_type=MESH)
        return carry

    lax.fori_loop(1, n, greet, 0)

    load_basis = pltpu.make_async_copy(zbasis_ref, zraw, local_sem.at[0])
    load_pack = pltpu.make_async_copy(pack_hbm, pack_ref, local_sem.at[1])
    load_basis.start()
    load_pack.start()

    def source(whose, piece):
        at = jnp.minimum(whose * (share * strip) + piece * SUB, width - SUB)
        return images_ref.at[:, :, pl.ds(pl.multiple_of(at, SUB), SUB)]

    def landing(whose, piece):
        if rows % 8:
            return pieces.at[whose, :, :, pl.ds(piece * SUB, SUB)]
        return strips.at[:, pl.ds(pl.multiple_of(whose * rows, 8), rows), pl.ds(piece * SUB, SUB)]

    own_copies = [
        pltpu.make_async_copy(source(place, piece), landing(place, piece), strip_local.at[piece])
        for piece in range(count)
    ]
    for copy in own_copies:
        copy.start()

    lane8 = lax.broadcasted_iota(jnp.int32, (8, SUB), 1)
    row8 = lax.broadcasted_iota(jnp.int32, (8, SUB), 0)
    message = jnp.zeros((8, SUB), F32)
    for t in range(TR):
        anchor = anchors_ref[t].astype(F32)
        patch = patches_ref[t].astype(F32)
        message = jnp.where((row8 == t) & (lane8 >= SLOT), anchor, message)
        message = jnp.where(row8 == TR + t, patch, message)
    tile_ref[...] = message
    modes = coeffs_ref.shape[2]
    for f in range(FRAMES):
        tile_ref[f : f + 1, :modes] = coeffs_ref[f]
    everyone[me] = tile_ref[...]

    load_basis.wait()
    zpad[...] = jnp.zeros(zpad.shape, F32)
    zpad[:modes] = zraw[...]
    ztable[...] = jnp.zeros(ztable.shape, BF16)
    basis_high, basis_low = split(zpad[...])
    ztable[:MODE_ROWS] = basis_high
    ztable[MODE_ROWS : 2 * MODE_ROWS] = basis_low
    ztable[SUB : SUB + MODE_ROWS] = basis_high

    pl.semaphore_wait(barrier, n - 1)

    def spread(block_ref, out_ref, stage, step):
        return pltpu.make_async_remote_copy(
            src_ref=block_ref,
            dst_ref=out_ref.at[me],
            send_sem=send_sem.at[stage],
            recv_sem=recv_sem.at[stage],
            device_id=(lax.rem(me + step, n),),
            device_id_type=MESH,
        )

    def begin_all(block_ref, out_ref, stage):
        def begin(step, carry):
            spread(block_ref, out_ref, stage, step).start()
            return carry

        lax.fori_loop(1, n, begin, 0)

    def finish_all(out_ref, stage):
        part = out_ref.at[pl.ds(0, n - 1)]
        pltpu.make_async_copy(part, part, recv_sem.at[stage]).wait()

    begin_all(tile_ref, everyone, 0)

    def send_strip(piece, step):
        whose = lax.rem(place + step, team)
        return pltpu.make_async_remote_copy(
            src_ref=source(whose, piece),
            dst_ref=landing(place, piece),
            send_sem=strip_send.at[0],
            recv_sem=strip_recv.at[piece],
            device_id=(tile * team + whose,),
            device_id_type=MESH,
        )

    for piece in range(count):

        def begin_strip(step, carry, piece=piece):
            send_strip(piece, step).start()
            return carry

        lax.fori_loop(1, team, begin_strip, 0)

    finish_all(everyone, 0)

    low_rows, low_lanes = row8 < TR, lane8 < SLOT

    def patch_row(home, t):
        return everyone[home, pl.ds(TR + t, 1), :]

    def note_owner(device, carry):
        their_tile = device // team
        base = share * lax.rem(device, team)
        line = [patch_row(base + k, their_tile) for k in range(share)]
        owners[device] = jnp.where(
            low_rows, jnp.where(low_lanes, line[0], line[2]), jnp.where(low_lanes, line[1], line[3])
        )
        return carry

    lax.fori_loop(0, n, note_owner, 0)
    for k in range(share):
        wanted[k] = jnp.broadcast_to(patch_row(share * place + k, tile), (8, SUB))
    wanted[share] = jnp.full((8, SUB), 1.0, F32) * me.astype(F32)

    def gather_coeffs(device, sums):
        block = everyone[device]
        number = device.astype(F32)
        return tuple(s + jnp.where(wanted[k] == number, block, 0.0) for k, s in enumerate(sums))

    zero8 = jnp.zeros((8, SUB), F32)
    found = lax.fori_loop(0, n, gather_coeffs, (zero8,) * share)
    for k in range(share):
        current[k * FRAMES : (k + 1) * FRAMES, :] = jnp.where(low_lanes, found[k], 0.0)[:FRAMES]
    current[share * FRAMES : (share + 1) * FRAMES, :] = jnp.where(low_lanes, tile_ref[...], 0.0)[:FRAMES]

    load_pack.wait()
    forward_tables = views(pack_ref, spots, *FORWARD)
    backward_tables = views(pack_ref, spots, *BACKWARD)
    data_tables = views(pack_ref, spots, *DATA)
    pixel_rows = PUP // 2
    chosen_rows = share * FRAMES

    def phases():
        value = current[:chosen_rows, :]
        lane = lax.broadcasted_iota(jnp.int32, value.shape, 1)
        high = value.astype(BF16).astype(F32)
        twice = jnp.where(lane < MODE_ROWS, high, pltpu.roll(high, MODE_ROWS, 1))
        left = jnp.concatenate([twice.astype(BF16), (value - high).astype(BF16)], 1)
        for c in range(0, pixel_rows, 2):
            phase = dot(left, ztable[:, c * SUB : (c + 2) * SUB])
            for half in range(2):
                for r in range(0, chosen_rows, 8):
                    phase_ref[pl.ds(r * pixel_rows + c + half, 8, stride=pixel_rows), :] = phase[
                        r : r + 8, half * SUB : (half + 1) * SUB
                    ]

    def window(k, lane, anchor, valid):
        shift = lax.rem(anchor, SUB)
        turn = lax.rem(SUB - shift, SUB)
        parts = []
        for cf in range(FIELDS):
            at = first[k] * SUB if isinstance(k, int) else pl.multiple_of(k * strip // SUB * SUB, SUB)
            one = pltpu.roll(strips[cf, :, pl.ds(at, SUB)], turn, 1)
            two = pltpu.roll(strips[cf, :, pl.ds(at + SUB, SUB)], turn, 1)
            parts.append(jnp.where(lane < SUB - shift, one, jnp.where(lane < valid, two, 0.0)))
        return jnp.concatenate(parts, 1)

    def forward(k, carry):
        otf, field, pupil = forward_math(
            scale, phase_ref[pl.ds(pl.multiple_of(k * SUB, SUB), SUB), :], fixed_ref, forward_tables
        )
        otf_ref[k] = otf
        field_ref[k] = field
        pupil_ref[k] = pupil
        return carry

    def backward(k, carry):
        total = backward_math(
            scale, data_ref[k], otf_ref[k], field_ref[k], pupil_ref[k], fixed_ref, backward_tables
        )
        total_ref[pl.ds(pl.multiple_of(k * SUB, SUB), SUB), :] = total
        return carry

    def wait_strip(piece):
        own_copies[piece].wait()
        if rows % 8:
            part = pieces.at[pl.ds(0, team - 1), :, :, pl.ds(piece * SUB, SUB)]
        else:
            part = strips.at[:, pl.ds(0, (team - 1) * rows), pl.ds(piece * SUB, SUB)]
        pltpu.make_async_copy(part, part, strip_recv.at[piece]).wait()
        if rows % 8:
            for q in range(team):
                strips[:, q * rows : (q + 1) * rows, piece * SUB : (piece + 1) * SUB] = pieces[
                    q, :, :, piece * SUB : (piece + 1) * SUB
                ]

    lane128 = lax.broadcasted_iota(jnp.int32, (SUB, SUB), 1)

    def take_data(k):
        anchor = jnp.max(everyone[share * place + k, pl.ds(tile, 1), SLOT:]).astype(jnp.int32)
        begin = (place * share + k) * strip // SUB * SUB
        valid = jnp.where(begin + SUB <= width - SUB, SUB, 0)
        data_ref[k] = half_plane(window(k, lane128, anchor, valid), *data_tables)

    def reduce_modes():
        block = jnp.concatenate(
            [total_ref[pl.ds(c, chosen_rows, stride=pixel_rows), :] for c in range(pixel_rows)], 1
        )
        both = jnp.concatenate(split(block), 0)
        result = lax.dot_general(
            both, ztable[:SUB], (((1,), (1,)), ((), ())), preferred_element_type=F32
        )
        high, low = result[:chosen_rows], result[chosen_rows:]
        lane = lax.broadcasted_iota(jnp.int32, high.shape, 1)
        slope = high + low + pltpu.roll(high, SUB - MODE_ROWS, 1)
        slope = jnp.where(lane < modes, slope, 0.0)
        return jnp.where(low_lanes, slope[:8], pltpu.roll(slope[8:], SLOT, 1))

    def fold(value):
        value = value + pltpu.roll(value, SLOT, 1)
        value = value + pltpu.roll(value, TR, 0)
        return jnp.where(low_lanes, value, 0.0)[:FRAMES]

    for iteration in range(ITERS):
        phases()
        lax.fori_loop(0, share, forward, 0)
        if iteration == 0:
            done = 0
            for k in range(share):
                while done <= first[k] + 1:
                    wait_strip(done)
                    done += 1
                take_data(k)
                backward(k, 0)
        else:
            lax.fori_loop(0, share, backward, 0)
        mine_ref[iteration] = reduce_modes()
        begin_all(mine_ref.at[iteration], slopes.at[iteration], 1 + iteration)
        slopes[iteration, me] = mine_ref[iteration]
        finish_all(slopes.at[iteration], 1 + iteration)

        def gather_slopes(device, sums, iteration=iteration):
            block = slopes[iteration, device]
            owner = owners[device]
            return tuple(s + jnp.where(owner == wanted[k], block, 0.0) for k, s in enumerate(sums))

        sums = lax.fori_loop(0, n, gather_slopes, (zero8,) * (share + 1))
        for k in range(share + 1):
            gradient = fold(sums[k])
            at = k * FRAMES
            current[at : at + FRAMES, :] = current[at : at + FRAMES, :] - STEP_SIZE * gradient
            if k == share and iteration == ITERS - 1:
                fresh = current[at : at + FRAMES, :]
                for f in range(FRAMES):
                    new_ref[f] = fresh[f : f + 1, :modes]
                    grad_ref[f] = gradient[f : f + 1, :modes]

    for stage, block in ((0, everyone), (1, slopes.at[0]), (2, slopes.at[1])):
        part = block.at[pl.ds(0, n - 1)]
        pltpu.make_async_copy(part, part, send_sem.at[stage]).wait()
    sent = images_ref.at[:, :, pl.ds(0, count * SUB)]
    for _ in range(team - 1):
        pltpu.make_async_copy(sent, sent, strip_send.at[0]).wait()


def on_device(images, anchors, patches, coeffs, zbasis):
    n = lax.axis_size("sub")
    rows, width = images.shape[2:]
    modes = coeffs.shape[1]
    tables = make_tables()
    pack, spots = pack_tables(tables)
    pack = jnp.asarray(pack)
    scale = float(1.0 / (SUB * SUB * tables["area"]))
    fixed = jnp.asarray(np.concatenate([tables["mask"], tables["weight"]], 0))
    team, share, strip, first, count = plan(n, width, rows)
    assert coeffs.shape[2] == 1 and anchors.shape[0] == 4 and share == 4
    pixels = zbasis.shape[1]
    piece_shape = (team, FIELDS, rows, count * SUB) if rows % 8 else (1, 1, 8, SUB)
    out_shape = jax.ShapeDtypeStruct((FRAMES, 1, modes), F32)
    anywhere = pl.BlockSpec(memory_space=pl.ANY)
    vmem = pl.BlockSpec(memory_space=pltpu.VMEM)
    smem = pl.BlockSpec(memory_space=pltpu.SMEM)
    new, gradient = pl.pallas_call(
        functools.partial(mega_kernel, scale, spots, n, width, rows),
        out_shape=[out_shape, out_shape],
        in_specs=[anywhere, smem, smem, vmem, anywhere, vmem, anywhere],
        out_specs=[vmem, vmem],
        scratch_shapes=[
            pltpu.VMEM((8, SUB), F32),
            pltpu.VMEM((n, 8, SUB), F32),
            pltpu.VMEM((n, 8, SUB), F32),
            pltpu.VMEM((FIELDS, SUB, count * SUB), F32),
            pltpu.VMEM(piece_shape, F32),
            pltpu.VMEM((modes, pixels), F32),
            pltpu.VMEM((MODE_ROWS, pixels), F32),
            pltpu.VMEM((2 * SUB, pixels), BF16),
            pltpu.VMEM(pack.shape, BF16),
            pltpu.VMEM((share * SUB, SUB), F32),
            pltpu.VMEM((share * SUB, SUB), F32),
            pltpu.VMEM((share, FIELDS * HALF, 2 * SUB), F32),
            pltpu.VMEM((share, 2 * SUB, FIELDS * SUB), F32),
            pltpu.VMEM((share, FIELDS * PUP // 2, 2 * SUB), F32),
            pltpu.VMEM((share, FIELDS * HALF, 2 * SUB), F32),
            pltpu.VMEM(((share + 1) * FRAMES + 4, SUB), F32),
            pltpu.VMEM((share + 1, 8, SUB), F32),
            pltpu.VMEM((ITERS, 8, SUB), F32),
            pltpu.VMEM((ITERS, n, 8, SUB), F32),
            pltpu.SemaphoreType.DMA((2,)),
            pltpu.SemaphoreType.DMA((1 + ITERS,)),
            pltpu.SemaphoreType.DMA((1 + ITERS,)),
            pltpu.SemaphoreType.DMA((1,)),
            pltpu.SemaphoreType.DMA((count,)),
            pltpu.SemaphoreType.DMA((count,)),
        ],
        compiler_params=pltpu.CompilerParams(
            collective_id=0, has_side_effects=True, vmem_limit_bytes=VMEM_LIMIT
        ),
    )(
        images.reshape(FIELDS, rows, width),
        anchors,
        patches,
        coeffs.transpose(0, 2, 1),
        zbasis,
        fixed,
        pack,
    )
    return new.transpose(0, 2, 1), gradient.transpose(0, 2, 1)


def solution(mesh):
    return jax.shard_map(
        on_device,
        mesh=mesh,
        in_specs=(P(None, None, "sub", None), P("sub"), P("sub"), P(None, None, "sub"), P()),
        out_specs=(P(None, None, "sub"), P(None, None, "sub")),
        check_vma=False,
    )
```

```python
import functools
import math

import jax
import jax.numpy as jnp
import ml_dtypes
import numpy as np
from jax import lax
from jax.experimental import pallas as pl
from jax.experimental.pallas import tpu as pltpu
from jax.sharding import PartitionSpec as P

SUB = 128
CH = 2
FRAMES = 4
FIELDS = CH * FRAMES
SLOT = 64
TR = 4
ITERS = 2
PUP = 64
HALF = 72
EVENS = 40
BAND = 32
GAMMA = 0.01
STEP_SIZE = 0.05
F32 = jnp.float32
BF16 = jnp.bfloat16
VMEM_LIMIT = 60 << 20
SIN = (-1.6666666e-1, 8.3333310e-3, -1.9840874e-4, 2.7525562e-6, -2.3889859e-8)
COS = (-0.5, 4.1666666e-2, -1.3888889e-3, 2.4801587e-5, -2.7557319e-7, 2.0876757e-9)


def split_np(matrix):
    matrix = np.asarray(matrix, np.float32)
    high = matrix.astype(ml_dtypes.bfloat16)
    low = (matrix - high.astype(np.float32)).astype(ml_dtypes.bfloat16)
    return high, low


def cos_sin(rows, columns):
    angle = 2.0 * np.pi * np.outer(rows, columns) / SUB
    return np.cos(angle), np.sin(angle)


def make_tables():
    k = np.arange(SUB)
    cos, sin = cos_sin(k, k)
    taper = 0.5 - 0.5 * np.cos(2.0 * np.pi * (k + 0.5) / SUB)
    centred = np.arange(PUP) - PUP / 2 + 0.5
    mask = (centred[:, None] ** 2 + centred[None, :] ** 2 <= (PUP / 2) ** 2).astype(np.float32)
    scale = 1.0 / (SUB * SUB * float(mask.sum()))
    c, s = cos[:PUP], sin[:PUP]
    right_even = np.block([[c, -s], [s, c]])
    right_odd = np.block([[-s, -c], [c, -s]])
    left = np.concatenate(cos_sin(k, centred[:BAND]), 1)
    even, odd = np.zeros((2 * EVENS, PUP)), np.zeros((PUP, PUP))
    even[:33], even[EVENS : EVENS + 33] = cos_sin(np.arange(0, 65, 2), np.arange(PUP))
    odd[:BAND], odd[BAND:] = cos_sin(np.arange(1, 64, 2), np.arange(PUP))
    mixed = np.block([[cos, -sin], [-sin, -cos]])
    weight = np.zeros((HALF, 1))
    weight[:33] = weight[EVENS:] = 2.0
    weight[0] = weight[32] = 1.0
    weight = np.broadcast_to(weight * (-2.0 / SUB**4), (HALF, SUB))
    rows_taper = np.broadcast_to(taper[:, None] / scale, (SUB, SUB))
    packed_mask = np.concatenate([mask[:BAND], mask[::-1][:BAND]], 1)
    fixed = np.concatenate([packed_mask, weight, rows_taper], 0).astype(np.float32)
    matrices = {
        "right_even": (right_even, "down"),
        "right_odd": (right_odd, "down"),
        "left": (left, "across"),
        "even": (even * scale, "across"),
        "odd": (odd * scale, "across"),
        "mixed": (mixed, "down"),
        "data_mixed": (np.concatenate([taper, taper])[:, None] * mixed, "down"),
        "even_t": (even.T * (2.0 * scale), "across"),
        "odd_t": (odd.T * (2.0 * scale), "across"),
        "left_t": (left.T, "across"),
        "right_even_t": (right_even.T, "square"),
        "right_odd_t": (right_odd.T, "square"),
    }
    return matrices, fixed


def pack_tables(matrices):
    spots, parts, at = {}, [], 0
    width = 3 * SUB
    for name, (matrix, form) in matrices.items():
        high, low = split_np(matrix)
        if form == "square":
            part = np.block([[high, low], [high, np.zeros_like(low)]])
        else:
            part = np.concatenate([high, high, low], 0 if form == "down" else 1)
        spots[name] = (at, part.shape[0], part.shape[1])
        parts.append(np.pad(part, ((0, -part.shape[0] % 16), (0, width - part.shape[1]))))
        at += parts[-1].shape[0]
    return np.concatenate(parts, 0), spots


class Tables:
    def __init__(self, ref, spots):
        self.ref, self.spots = ref, spots

    def __getitem__(self, name):
        at, height, width = self.spots[name]
        return self.ref[at : at + height, :width]


def split(value):
    high = value.astype(BF16)
    low = (value - high.astype(F32)).astype(BF16)
    return high, low


def dot(a, b):
    return jnp.dot(a, b, preferred_element_type=F32)


def left_mul(table, value):
    high, low = split(value)
    return dot(table, jnp.concatenate([high, low, high], 0))


def right_mul(value, table):
    high, low = split(value)
    return dot(jnp.concatenate([high, low, high], 1), table)


def right_mul_narrow(value, table):
    both = dot(jnp.concatenate(split(value), 1), table)
    return both[:, :SUB] + both[:, SUB:]


def masked_cos_sin(angle, mask):
    turns = jnp.floor(angle * np.float32(1.0 / math.pi) + 0.5)
    rest = angle - turns * np.float32(3.140625)
    rest = rest - turns * np.float32(9.67025756835937500e-4)
    rest = rest - turns * np.float32(6.2771141529083252e-7)
    square = rest * rest
    sine = SIN[-1]
    for term in SIN[-2::-1]:
        sine = sine * square + term
    sine = rest + rest * (square * sine)
    cosine = COS[-1]
    for term in COS[-2::-1]:
        cosine = cosine * square + term
    cosine = 1.0 + square * cosine
    sign = mask - (2.0 * mask) * (turns - 2.0 * jnp.floor(turns * 0.5))
    return cosine * sign, sine * sign


def fields_of(value):
    return [value[:, f * SUB : (f + 1) * SUB] for f in range(FIELDS)]


def half_plane(images, tables, mixed):
    upper = jnp.concatenate([image[:PUP] + image[PUP:] for image in images], 1)
    lower = jnp.concatenate([image[:PUP] - image[PUP:] for image in images], 1)
    evens = left_mul(tables["even"], upper)
    odds = left_mul(tables["odd"], lower)
    stacked = [
        jnp.concatenate(
            [
                jnp.concatenate([even[:EVENS], odd[:BAND]], 0),
                jnp.concatenate([even[EVENS:], odd[BAND:]], 0),
            ],
            1,
        )
        for even, odd in zip(fields_of(evens), fields_of(odds))
    ]
    return right_mul(jnp.concatenate(stacked, 0), mixed)


def swap(value):
    return pltpu.roll(value, PUP, 1)


def forward_math(phase, fixed_ref, tables):
    phase = jnp.concatenate([phase * np.float32(1.0 / (1.0 + 0.25 * c)) for c in range(CH)], 0)
    mask = jnp.concatenate([fixed_ref[:BAND]] * FIELDS, 0)
    cosine, sine = masked_cos_sin(phase, mask)
    low = lax.broadcasted_iota(jnp.int32, cosine.shape, 1) < PUP
    top = jnp.where(low, cosine, swap(sine))
    bottom = jnp.where(low, swap(cosine), sine)
    even = right_mul(top + bottom, tables["right_even"])
    odd = right_mul(top - bottom, tables["right_odd"])
    blocks = jnp.concatenate(
        [
            jnp.concatenate([part[f * BAND : (f + 1) * BAND] for part in (even, odd)], 0)
            for f in range(FIELDS)
        ],
        1,
    )
    field = left_mul(tables["left"], blocks)
    images = []
    for f in range(FIELDS):
        real = field[:, 2 * f * SUB : (2 * f + 1) * SUB]
        imag = field[:, (2 * f + 1) * SUB : (2 * f + 2) * SUB]
        images.append(real * real + imag * imag)
    return half_plane(images, tables, tables["mixed"]), field, top, bottom


def backward_math(data, otf, field, top, bottom, fixed_ref, tables):
    weight = fixed_ref[BAND : BAND + HALF]
    bars = []
    for c in range(CH):
        parts = []
        cross_real = cross_imag = power = None
        for f in range(c * FRAMES, (c + 1) * FRAMES):
            d, o = data[f * HALF : (f + 1) * HALF], otf[f * HALF : (f + 1) * HALF]
            dr, di, orr, oi = d[:, :SUB], d[:, SUB:], o[:, :SUB], o[:, SUB:]
            parts.append((dr, di, orr, oi))
            terms = (dr * orr + di * oi, di * orr - dr * oi, orr * orr + oi * oi)
            if cross_real is None:
                cross_real, cross_imag, power = terms
            else:
                cross_real = cross_real + terms[0]
                cross_imag = cross_imag + terms[1]
                power = power + terms[2]
        inverse = 1.0 / (power + GAMMA)
        slope = weight * inverse
        xr, xi = cross_real * inverse, cross_imag * inverse
        share = weight * (xr * xr + xi * xi)
        cross_real, cross_imag = cross_real * slope, cross_imag * slope
        for dr, di, orr, oi in parts:
            bar_real = cross_real * dr + cross_imag * di - share * orr
            bar_imag = cross_real * di - cross_imag * dr - share * oi
            bars.append(jnp.concatenate([bar_real, bar_imag], 1))
    columns = right_mul(jnp.concatenate(bars, 0), tables["mixed"])
    evens, odds = [], []
    for f in range(FIELDS):
        part = columns[f * HALF : (f + 1) * HALF]
        evens.append(jnp.concatenate([part[:EVENS, :SUB], part[:EVENS, SUB:]], 0))
        odds.append(jnp.concatenate([part[EVENS:, :SUB], part[EVENS:, SUB:]], 0))
    even = left_mul(tables["even_t"], jnp.concatenate(evens, 1))
    odd = left_mul(tables["odd_t"], jnp.concatenate(odds, 1))
    psf_bar = fields_of(jnp.concatenate([even + odd, even - odd], 0))
    field_bar = jnp.concatenate(
        [field[:, (2 * f + part) * SUB : (2 * f + part + 1) * SUB] * psf_bar[f] for f in range(FIELDS) for part in (0, 1)],
        1,
    )
    half_bar = left_mul(tables["left_t"], field_bar)
    pieces = [half_bar[:, 2 * f * SUB : (2 * f + 2) * SUB] for f in range(FIELDS)]
    even_bar = right_mul_narrow(jnp.concatenate([p[:BAND] for p in pieces], 0), tables["right_even_t"])
    odd_bar = right_mul_narrow(jnp.concatenate([p[BAND:] for p in pieces], 0), tables["right_odd_t"])
    size = FRAMES * BAND
    sums = []
    for pupil, bar in ((top, even_bar + odd_bar), (bottom, even_bar - odd_bar)):
        product = pupil * swap(bar)
        total = product[:size]
        for c in range(1, CH):
            total = total + product[c * size : (c + 1) * size] * np.float32(1.0 / (1.0 + 0.25 * c))
        sums.append(total)
    low = lax.broadcasted_iota(jnp.int32, sums[0].shape, 1) < PUP
    return jnp.where(low, sums[0] - swap(sums[0]), swap(sums[1]) - sums[1])


MODE_ROWS = 48
MESH = pl.DeviceIdType.MESH


def plan(n, width, rows):
    team = n // TR
    share = n * 4 // TR // team
    strip = width * TR // (n * 4)
    first = [k * strip // SUB for k in range(share)]
    return team, share, strip, first, share * strip // SUB + 1


def mega_kernel(
    spots,
    n,
    width,
    rows,
    images_ref,
    anchors_hbm,
    patches_hbm,
    coeffs_hbm,
    zbasis_ref,
    fixed_hbm,
    pack_hbm,
    new_ref,
    grad_ref,
    anchors_ref,
    patches_ref,
    coeffs_ref,
    fixed_ref,
    tile_ref,
    everyone,
    owners,
    strips,
    pieces,
    zraw,
    zpad,
    ztable,
    pack_ref,
    phase_ref,
    total_ref,
    otf_ref,
    field_ref,
    pupil_ref,
    data_ref,
    current,
    wanted,
    mine_ref,
    slopes,
    local_sem,
    send_sem,
    recv_sem,
    strip_send,
    strip_recv,
    strip_local,
    hand_send,
    hand_recv,
):
    me = lax.axis_index("sub")
    team, share, strip, first, count = plan(n, width, rows)
    tile = me // team
    place = lax.rem(me, team)
    barrier = pltpu.get_barrier_semaphore()

    far = tile // 2
    planes = [3 - 3 * far, 2 - far, tile + 1 - 2 * lax.rem(tile, 2), tile]
    for plane in planes:

        def greet(step, carry, plane=plane):
            whom = plane * team + lax.rem(place + step, team)
            pl.semaphore_signal(barrier, inc=1, device_id=(whom,), device_id_type=MESH)
            return carry

        lax.fori_loop(1 if plane is tile else 0, team, greet, 0)

    load_anchors = pltpu.make_async_copy(anchors_hbm, anchors_ref, local_sem.at[2])
    load_patches = pltpu.make_async_copy(patches_hbm, patches_ref, local_sem.at[3])
    load_coeffs = pltpu.make_async_copy(coeffs_hbm, coeffs_ref, local_sem.at[4])
    load_fixed = pltpu.make_async_copy(fixed_hbm, fixed_ref, local_sem.at[5])
    load_basis = pltpu.make_async_copy(zbasis_ref, zraw, local_sem.at[0])
    load_pack = pltpu.make_async_copy(pack_hbm, pack_ref, local_sem.at[1])
    for load in (load_anchors, load_patches, load_coeffs, load_fixed, load_basis, load_pack):
        load.start()

    def source(whose, piece):
        at = jnp.minimum(whose * (share * strip) + piece * SUB, width - SUB)
        return images_ref.at[:, :, pl.ds(pl.multiple_of(at, SUB), SUB)]

    def landing(whose, piece):
        if rows % 8:
            return pieces.at[whose, :, :, pl.ds(piece * SUB, SUB)]
        return strips.at[:, pl.ds(pl.multiple_of(whose * rows, 8), rows), pl.ds(piece * SUB, SUB)]

    last = count - 1
    odd = lax.rem(place, 2) == 1
    reaches = odd & (place != team - 1)

    def own_copy(piece):
        return pltpu.make_async_copy(source(place, piece), landing(place, piece), strip_local.at[piece])

    for piece in range(last):
        own_copy(piece).start()

    @pl.when(reaches)
    def _():
        own_copy(last).start()

    load_anchors.wait()
    load_patches.wait()
    load_coeffs.wait()
    lane8 = lax.broadcasted_iota(jnp.int32, (8, SUB), 1)
    row8 = lax.broadcasted_iota(jnp.int32, (8, SUB), 0)
    message = jnp.zeros((8, SUB), F32)
    for t in range(TR):
        anchor = anchors_ref[t].astype(F32)
        patch = patches_ref[t].astype(F32)
        message = jnp.where((row8 == t) & (lane8 >= SLOT), anchor, message)
        message = jnp.where(row8 == TR + t, patch, message)
    tile_ref[...] = message
    modes = coeffs_ref.shape[2]
    for f in range(FRAMES):
        tile_ref[f : f + 1, :modes] = coeffs_ref[f]
    everyone[me] = tile_ref[...]

    pl.semaphore_wait(barrier, n - 1)

    def spread(block_ref, out_ref, stage, target):
        return pltpu.make_async_remote_copy(
            src_ref=block_ref,
            dst_ref=out_ref.at[me],
            send_sem=send_sem.at[stage],
            recv_sem=recv_sem.at[stage],
            device_id=(target,),
            device_id_type=MESH,
        )

    def begin_all(block_ref, out_ref, stage):
        for plane in planes:

            def begin(step, carry, plane=plane):
                spread(block_ref, out_ref, stage, plane * team + lax.rem(place + step, team)).start()
                return carry

            lax.fori_loop(1 if plane is tile else 0, team, begin, 0)

    def finish_all(out_ref, stage):
        part = out_ref.at[pl.ds(0, n - 1)]
        pltpu.make_async_copy(part, part, recv_sem.at[stage]).wait()

    begin_all(tile_ref, everyone, 0)

    def send_strip(piece, whose):
        return pltpu.make_async_remote_copy(
            src_ref=source(whose, piece),
            dst_ref=landing(place, piece),
            send_sem=strip_send.at[piece // last],
            recv_sem=strip_recv.at[piece],
            device_id=(tile * team + whose,),
            device_id_type=MESH,
        )

    for piece in range(last):

        def begin_strip(step, carry, piece=piece):
            send_strip(piece, lax.rem(place + step, team)).start()
            return carry

        lax.fori_loop(1, team, begin_strip, 0)

    def begin_last(i, carry):
        @pl.when(2 * i + 1 != place)
        def _():
            send_strip(last, 2 * i + 1).start()

        return carry

    lax.fori_loop(0, team // 2 - 1, begin_last, 0)

    def hand_on():
        return pltpu.make_async_remote_copy(
            src_ref=strips.at[:, :, pl.ds(0, SUB)],
            dst_ref=strips.at[:, :, pl.ds(last * SUB, SUB)],
            send_sem=hand_send.at[0],
            recv_sem=hand_recv.at[0],
            device_id=(me - 1,),
            device_id_type=MESH,
        )

    load_basis.wait()
    zpad[...] = jnp.zeros(zpad.shape, F32)
    zpad[:modes] = zraw[...]
    ztable[...] = jnp.zeros(ztable.shape, BF16)
    low48 = lax.broadcasted_iota(jnp.int32, (MODE_ROWS, SUB), 1) < PUP
    for i in range(0, BAND, 2):
        one, two = (zpad[:, c * SUB : (c + 1) * SUB] for c in (i // 2, BAND - 1 - i // 2))
        for j in range(2):
            basis_high, basis_low = split(jnp.where(low48, one, two))
            spot = slice((i + j) * SUB, (i + j + 1) * SUB)
            ztable[:MODE_ROWS, spot] = basis_high
            ztable[MODE_ROWS : 2 * MODE_ROWS, spot] = basis_low
            ztable[SUB : SUB + MODE_ROWS, spot] = basis_high
            one, two = swap(one), swap(two)

    finish_all(everyone, 0)

    low_rows, low_lanes = row8 < TR, lane8 < SLOT

    def patch_row(home, t):
        return everyone[home, pl.ds(TR + t, 1), :]

    def note_owner(device, carry):
        their_tile = device // team
        base = share * lax.rem(device, team)
        line = [patch_row(base + k, their_tile) for k in range(share)]
        owners[device] = jnp.where(
            low_rows, jnp.where(low_lanes, line[0], line[2]), jnp.where(low_lanes, line[1], line[3])
        )
        return carry

    def by_device(body, start):
        def block(i, carry):
            for j in range(8):
                carry = body(i * 8 + j, carry)
            return carry

        return lax.fori_loop(0, n // 8, block, start)

    by_device(note_owner, 0)
    for k in range(share):
        wanted[k] = jnp.broadcast_to(patch_row(share * place + k, tile), (8, SUB))
    wanted[share] = jnp.full((8, SUB), 1.0, F32) * me.astype(F32)

    def gather_coeffs(device, sums):
        block = everyone[device]
        number = device.astype(F32)
        return tuple(s + jnp.where(wanted[k] == number, block, 0.0) for k, s in enumerate(sums))

    zero8 = jnp.zeros((8, SUB), F32)
    found = by_device(gather_coeffs, (zero8,) * share)
    for k in range(share):
        current[k * FRAMES : (k + 1) * FRAMES, :] = jnp.where(low_lanes, found[k], 0.0)[:FRAMES]
    current[share * FRAMES : (share + 1) * FRAMES, :] = jnp.where(low_lanes, tile_ref[...], 0.0)[:FRAMES]

    load_pack.wait()
    load_fixed.wait()
    tables = Tables(pack_ref, spots)
    pixel_rows = PUP // 2
    chosen_rows = share * FRAMES

    def phases():
        value = current[:chosen_rows, :]
        lane = lax.broadcasted_iota(jnp.int32, value.shape, 1)
        high = value.astype(BF16).astype(F32)
        twice = jnp.where(lane < MODE_ROWS, high, pltpu.roll(high, MODE_ROWS, 1))
        left = jnp.concatenate([twice.astype(BF16), (value - high).astype(BF16)], 1)
        for c in range(0, pixel_rows, 2):
            phase = dot(left, ztable[:, c * SUB : (c + 2) * SUB])
            for half in range(2):
                for r in range(0, chosen_rows, 8):
                    phase_ref[pl.ds(r * pixel_rows + c + half, 8, stride=pixel_rows), :] = phase[
                        r : r + 8, half * SUB : (half + 1) * SUB
                    ]

    def window(k, lane, anchor, valid):
        shift = lax.rem(anchor, SUB)
        turn = lax.rem(SUB - shift, SUB)
        parts = []
        for cf in range(FIELDS):
            at = first[k] * SUB if isinstance(k, int) else pl.multiple_of(k * strip // SUB * SUB, SUB)
            one = pltpu.roll(strips[cf, :, pl.ds(at, SUB)], turn, 1)
            two = pltpu.roll(strips[cf, :, pl.ds(at + SUB, SUB)], turn, 1)
            cut = jnp.where(lane < SUB - shift, one, jnp.where(lane < valid, two, 0.0))
            parts.append(cut * fixed_ref[BAND + HALF :])
        return parts

    def forward(k, carry):
        at = k * SUB if isinstance(k, int) else pl.multiple_of(k * SUB, SUB)
        otf, field, top, bottom = forward_math(phase_ref[pl.ds(at, SUB), :], fixed_ref, tables)
        otf_ref[k] = otf
        field_ref[k] = field
        pupil_ref[k, 0] = top
        pupil_ref[k, 1] = bottom
        return carry

    def backward(k, carry):
        total = backward_math(
            data_ref[k], otf_ref[k], field_ref[k], pupil_ref[k, 0], pupil_ref[k, 1], fixed_ref, tables
        )
        at = k * SUB if isinstance(k, int) else pl.multiple_of(k * SUB, SUB)
        total_ref[pl.ds(at, SUB), :] = total
        return carry

    def wait_piece(piece):
        own_copy(piece).wait()
        if rows % 8:
            part = pieces.at[pl.ds(0, team - 1), :, :, pl.ds(piece * SUB, SUB)]
        else:
            part = strips.at[:, pl.ds(0, (team - 1) * rows), pl.ds(piece * SUB, SUB)]
        pltpu.make_async_copy(part, part, strip_recv.at[piece]).wait()
        if rows % 8:
            for q in range(team):
                strips[:, q * rows : (q + 1) * rows, piece * SUB : (piece + 1) * SUB] = pieces[
                    q, :, :, piece * SUB : (piece + 1) * SUB
                ]

    def wait_strip(piece):
        if piece == last:

            @pl.when(reaches)
            def _():
                wait_piece(last)

            @pl.when(jnp.logical_not(odd))
            def _():
                whole_strip = strips.at[:, :, pl.ds(last * SUB, SUB)]
                pltpu.make_async_copy(whole_strip, whole_strip, hand_recv.at[0]).wait()

        else:
            wait_piece(piece)
        if piece == 0:

            @pl.when(odd)
            def _():
                hand_on().start()

    lane128 = lax.broadcasted_iota(jnp.int32, (SUB, SUB), 1)

    def take_data(k):
        anchor = jnp.max(everyone[share * place + k, pl.ds(tile, 1), SLOT:]).astype(jnp.int32)
        begin = (place * share + k) * strip // SUB * SUB
        valid = jnp.where(begin + SUB <= width - SUB, SUB, 0)
        data_ref[k] = half_plane(window(k, lane128, anchor, valid), tables, tables["data_mixed"])

    def reduce_modes():
        block = jnp.concatenate(
            [total_ref[pl.ds(c, chosen_rows, stride=pixel_rows), :] for c in range(pixel_rows)], 1
        )
        both = jnp.concatenate(split(block), 0)
        result = lax.dot_general(
            both, ztable[:SUB], (((1,), (1,)), ((), ())), preferred_element_type=F32
        )
        high, low = result[:chosen_rows], result[chosen_rows:]
        lane = lax.broadcasted_iota(jnp.int32, high.shape, 1)
        slope = high + low + pltpu.roll(high, SUB - MODE_ROWS, 1)
        slope = jnp.where(lane < modes, slope, 0.0)
        return jnp.where(low_lanes, slope[:8], pltpu.roll(slope[8:], SLOT, 1))

    def fold(value):
        value = value + pltpu.roll(value, SLOT, 1)
        value = value + pltpu.roll(value, TR, 0)
        return jnp.where(low_lanes, value, 0.0)[:FRAMES]

    for iteration in range(ITERS):
        phases()
        if iteration == 0:
            lax.fori_loop(0, share, forward, 0)
        else:
            forward(0, 0)
        if iteration == 0:
            done = 0
            for k in range(share):
                while done <= first[k] + 1:
                    wait_strip(done)
                    done += 1
                take_data(k)
                backward(k, 0)
        else:
            for k in range(share):
                if k + 1 < share:
                    forward(k + 1, 0)
                backward(k, 0)
        mine_ref[iteration] = reduce_modes()
        begin_all(mine_ref.at[iteration], slopes.at[iteration], 1 + iteration)
        slopes[iteration, me] = mine_ref[iteration]
        finish_all(slopes.at[iteration], 1 + iteration)

        def gather_slopes(device, sums, iteration=iteration):
            block = slopes[iteration, device]
            owner = owners[device]
            return tuple(s + jnp.where(owner == wanted[k], block, 0.0) for k, s in enumerate(sums))

        sums = by_device(gather_slopes, (zero8,) * (share + 1))
        for k in range(share + 1):
            gradient = fold(sums[k])
            at = k * FRAMES
            current[at : at + FRAMES, :] = current[at : at + FRAMES, :] - STEP_SIZE * gradient
            if k == share and iteration == ITERS - 1:
                fresh = current[at : at + FRAMES, :]
                for f in range(FRAMES):
                    new_ref[f] = fresh[f : f + 1, :modes]
                    grad_ref[f] = gradient[f : f + 1, :modes]

    for stage, block in ((0, everyone), (1, slopes.at[0]), (2, slopes.at[1])):
        part = block.at[pl.ds(0, n - 1)]
        pltpu.make_async_copy(part, part, send_sem.at[stage]).wait()
    sent = images_ref.at[:, :, pl.ds(0, last * SUB)]
    for _ in range(team - 1):
        pltpu.make_async_copy(sent, sent, strip_send.at[0]).wait()

    def finish_last(i, carry):
        @pl.when(2 * i + 1 != place)
        def _():
            send_strip(last, 2 * i + 1).wait_send()

        return carry

    lax.fori_loop(0, team // 2 - 1, finish_last, 0)

    @pl.when(odd)
    def _():
        hand_on().wait_send()


def on_device(images, anchors, patches, coeffs, zbasis):
    n = lax.axis_size("sub")
    rows, width = images.shape[2:]
    modes = coeffs.shape[1]
    matrices, fixed = make_tables()
    pack, spots = pack_tables(matrices)
    pack, fixed = jnp.asarray(pack), jnp.asarray(fixed)
    team, share, strip, first, count = plan(n, width, rows)
    assert coeffs.shape[2] == 1 and anchors.shape[0] == 4 and share == 4
    pixels = zbasis.shape[1]
    piece_shape = (team, FIELDS, rows, count * SUB) if rows % 8 else (1, 1, 8, SUB)
    out_shape = jax.ShapeDtypeStruct((FRAMES, 1, modes), F32)
    anywhere = pl.BlockSpec(memory_space=pl.ANY)
    vmem = pl.BlockSpec(memory_space=pltpu.VMEM)
    new, gradient = pl.pallas_call(
        functools.partial(mega_kernel, spots, n, width, rows),
        out_shape=[out_shape, out_shape],
        in_specs=[anywhere] * 7,
        out_specs=[vmem, vmem],
        scratch_shapes=[
            pltpu.SMEM(anchors.shape, jnp.int32),
            pltpu.SMEM(patches.shape, jnp.int32),
            pltpu.VMEM((FRAMES, 1, modes), F32),
            pltpu.VMEM(fixed.shape, F32),
            pltpu.VMEM((8, SUB), F32),
            pltpu.VMEM((n, 8, SUB), F32),
            pltpu.VMEM((n, 8, SUB), F32),
            pltpu.VMEM((FIELDS, SUB, count * SUB), F32),
            pltpu.VMEM(piece_shape, F32),
            pltpu.VMEM((modes, pixels), F32),
            pltpu.VMEM((MODE_ROWS, pixels), F32),
            pltpu.VMEM((2 * SUB, pixels), BF16),
            pltpu.VMEM(pack.shape, BF16),
            pltpu.VMEM((share * SUB, SUB), F32),
            pltpu.VMEM((share * SUB, SUB), F32),
            pltpu.VMEM((share, FIELDS * HALF, 2 * SUB), F32),
            pltpu.VMEM((share, SUB, 2 * FIELDS * SUB), F32),
            pltpu.VMEM((share, 2, FIELDS * BAND, SUB), F32),
            pltpu.VMEM((share, FIELDS * HALF, 2 * SUB), F32),
            pltpu.VMEM(((share + 1) * FRAMES + 4, SUB), F32),
            pltpu.VMEM((share + 1, 8, SUB), F32),
            pltpu.VMEM((ITERS, 8, SUB), F32),
            pltpu.VMEM((ITERS, n, 8, SUB), F32),
            pltpu.SemaphoreType.DMA((6,)),
            pltpu.SemaphoreType.DMA((1 + ITERS,)),
            pltpu.SemaphoreType.DMA((1 + ITERS,)),
            pltpu.SemaphoreType.DMA((2,)),
            pltpu.SemaphoreType.DMA((count,)),
            pltpu.SemaphoreType.DMA((count,)),
            pltpu.SemaphoreType.DMA((1,)),
            pltpu.SemaphoreType.DMA((1,)),
        ],
        compiler_params=pltpu.CompilerParams(
            collective_id=0, has_side_effects=True, vmem_limit_bytes=VMEM_LIMIT
        ),
    )(
        images.reshape(FIELDS, rows, width),
        anchors,
        patches,
        coeffs.transpose(0, 2, 1),
        zbasis,
        fixed,
        pack,
    )
    return new.transpose(0, 2, 1), gradient.transpose(0, 2, 1)


def solution(mesh):
    return jax.shard_map(
        on_device,
        mesh=mesh,
        in_specs=(P(None, None, "sub", None), P("sub"), P("sub"), P(None, None, "sub"), P()),
        out_specs=(P(None, None, "sub"), P(None, None, "sub")),
        check_vma=False,
    )
```

```python
import functools
import math

import jax
import jax.numpy as jnp
import ml_dtypes
import numpy as np
from jax import lax
from jax.experimental import pallas as pl
from jax.experimental.pallas import tpu as pltpu
from jax.sharding import PartitionSpec as P

SUB = 128
CH = 2
FRAMES = 4
FIELDS = CH * FRAMES
SLOT = 64
TR = 4
ITERS = 2
PUP = 64
HALF = 72
EVENS = 40
BAND = 32
GAMMA = 0.01
STEP_SIZE = 0.05
F32 = jnp.float32
BF16 = jnp.bfloat16
VMEM_LIMIT = 60 << 20
SIN = (-1.6666666e-1, 8.3333310e-3, -1.9840874e-4, 2.7525562e-6, -2.3889859e-8)
COS = (-0.5, 4.1666666e-2, -1.3888889e-3, 2.4801587e-5, -2.7557319e-7, 2.0876757e-9)


def split_np(matrix):
    matrix = np.asarray(matrix, np.float32)
    high = matrix.astype(ml_dtypes.bfloat16)
    low = (matrix - high.astype(np.float32)).astype(ml_dtypes.bfloat16)
    return high, low


def cos_sin(rows, columns):
    angle = 2.0 * np.pi * np.outer(rows, columns) / SUB
    return np.cos(angle), np.sin(angle)


def make_tables():
    k = np.arange(SUB)
    cos, sin = cos_sin(k, k)
    taper = 0.5 - 0.5 * np.cos(2.0 * np.pi * (k + 0.5) / SUB)
    centred = np.arange(PUP) - PUP / 2 + 0.5
    mask = (centred[:, None] ** 2 + centred[None, :] ** 2 <= (PUP / 2) ** 2).astype(np.float32)
    scale = 1.0 / (SUB * SUB * float(mask.sum()))
    c, s = cos[:PUP], sin[:PUP]
    right_even = np.block([[c, -s], [s, c]])
    right_odd = np.block([[-s, -c], [c, -s]])
    left = np.concatenate(cos_sin(k, centred[:BAND]), 1)
    even, odd = np.zeros((2 * EVENS, PUP)), np.zeros((PUP, PUP))
    even[:33], even[EVENS : EVENS + 33] = cos_sin(np.arange(0, 65, 2), np.arange(PUP))
    odd[:BAND], odd[BAND:] = cos_sin(np.arange(1, 64, 2), np.arange(PUP))
    mixed = np.block([[cos, -sin], [-sin, -cos]])
    weight = np.zeros((HALF, 1))
    weight[:33] = weight[EVENS:] = 2.0
    weight[0] = weight[32] = 1.0
    weight = np.broadcast_to(weight * (-2.0 / SUB**4), (HALF, SUB))
    rows_taper = np.broadcast_to(taper[:, None] / scale, (SUB, SUB))
    packed_mask = np.concatenate([mask[:BAND], mask[::-1][:BAND]], 1)
    fixed = np.concatenate([packed_mask, weight, rows_taper], 0).astype(np.float32)
    matrices = {
        "right_even": (right_even, "down"),
        "right_odd": (right_odd, "down"),
        "left": (left, "across"),
        "even": (even * scale, "across"),
        "odd": (odd * scale, "across"),
        "mixed": (mixed, "down"),
        "data_mixed": (np.concatenate([taper, taper])[:, None] * mixed, "down"),
        "even_t": (even.T * (2.0 * scale), "across"),
        "odd_t": (odd.T * (2.0 * scale), "across"),
        "left_t": (left.T, "across"),
        "right_even_t": (right_even.T, "square"),
        "right_odd_t": (right_odd.T, "square"),
    }
    return matrices, fixed


def pack_tables(matrices):
    spots, parts, at = {}, [], 0
    width = 3 * SUB
    for name, (matrix, form) in matrices.items():
        high, low = split_np(matrix)
        if form == "square":
            part = np.block([[high, low], [high, np.zeros_like(low)]])
        else:
            part = np.concatenate([high, high, low], 0 if form == "down" else 1)
        spots[name] = (at, part.shape[0], part.shape[1])
        parts.append(np.pad(part, ((0, -part.shape[0] % 16), (0, width - part.shape[1]))))
        at += parts[-1].shape[0]
    return np.concatenate(parts, 0), spots


class Tables:
    def __init__(self, ref, spots):
        self.ref, self.spots = ref, spots

    def __getitem__(self, name):
        at, height, width = self.spots[name]
        return self.ref[at : at + height, :width]


def split(value):
    high = value.astype(BF16)
    low = (value - high.astype(F32)).astype(BF16)
    return high, low


def dot(a, b):
    return jnp.dot(a, b, preferred_element_type=F32)


def left_mul(table, value):
    high, low = split(value)
    return dot(table, jnp.concatenate([high, low, high], 0))


def right_mul(value, table):
    high, low = split(value)
    return dot(jnp.concatenate([high, low, high], 1), table)


def right_mul_narrow(value, table):
    both = dot(jnp.concatenate(split(value), 1), table)
    return both[:, :SUB] + both[:, SUB:]


def masked_cos_sin(angle, mask):
    turns = jnp.floor(angle * np.float32(1.0 / math.pi) + 0.5)
    rest = angle - turns * np.float32(3.140625)
    rest = rest - turns * np.float32(9.67025756835937500e-4)
    rest = rest - turns * np.float32(6.2771141529083252e-7)
    square = rest * rest
    sine = SIN[-1]
    for term in SIN[-2::-1]:
        sine = sine * square + term
    sine = rest + rest * (square * sine)
    cosine = COS[-1]
    for term in COS[-2::-1]:
        cosine = cosine * square + term
    cosine = 1.0 + square * cosine
    sign = mask - (2.0 * mask) * (turns - 2.0 * jnp.floor(turns * 0.5))
    return cosine * sign, sine * sign


def fields_of(value):
    return [value[:, at : at + SUB] for at in range(0, value.shape[1], SUB)]


def interleave(*chains):
    results, live = [None] * len(chains), list(enumerate(chains))
    while live:
        still = []
        for at, chain in live:
            try:
                next(chain)
                still.append((at, chain))
            except StopIteration as stop:
                results[at] = stop.value
        live = still
    return results


def half_plane(images, tables, mixed):
    upper = jnp.concatenate([image[:PUP] + image[PUP:] for image in images], 1)
    lower = jnp.concatenate([image[:PUP] - image[PUP:] for image in images], 1)
    evens = left_mul(tables["even"], upper)
    odds = left_mul(tables["odd"], lower)
    stacked = [
        jnp.concatenate(
            [
                jnp.concatenate([even[:EVENS], odd[:BAND]], 0),
                jnp.concatenate([even[EVENS:], odd[BAND:]], 0),
            ],
            1,
        )
        for even, odd in zip(fields_of(evens), fields_of(odds))
    ]
    yield
    return right_mul(jnp.concatenate(stacked, 0), mixed)


def swap(value):
    return pltpu.roll(value, PUP, 1)


def forward_channel(phase, c, fixed_ref, tables):
    if c:
        phase = phase * np.float32(1.0 / (1.0 + 0.25 * c))
    mask = jnp.concatenate([fixed_ref[:BAND]] * FRAMES, 0)
    cosine, sine = masked_cos_sin(phase, mask)
    low = lax.broadcasted_iota(jnp.int32, cosine.shape, 1) < PUP
    top = jnp.where(low, cosine, swap(sine))
    bottom = jnp.where(low, swap(cosine), sine)
    even = right_mul(top + bottom, tables["right_even"])
    odd = right_mul(top - bottom, tables["right_odd"])
    yield
    blocks = jnp.concatenate(
        [
            jnp.concatenate([part[f * BAND : (f + 1) * BAND] for part in (even, odd)], 0)
            for f in range(FRAMES)
        ],
        1,
    )
    field = left_mul(tables["left"], blocks)
    yield
    images = []
    for f in range(FRAMES):
        real = field[:, 2 * f * SUB : (2 * f + 1) * SUB]
        imag = field[:, (2 * f + 1) * SUB : (2 * f + 2) * SUB]
        images.append(real * real + imag * imag)
    otf = yield from half_plane(images, tables, tables["mixed"])
    yield
    return otf, field, top, bottom


def join_channels(parts):
    sums = parts[0]
    for c in range(1, CH):
        ratio = np.float32(1.0 / (1.0 + 0.25 * c))
        sums = [a + b * ratio for a, b in zip(sums, parts[c])]
    low = lax.broadcasted_iota(jnp.int32, sums[0].shape, 1) < PUP
    return jnp.where(low, sums[0] - swap(sums[0]), swap(sums[1]) - sums[1])


def backward_channel(data, otf, field, top, bottom, fixed_ref, tables):
    weight = fixed_ref[BAND : BAND + HALF]
    parts, bars = [], []
    cross_real = cross_imag = power = None
    for f in range(FRAMES):
        d, o = data[f * HALF : (f + 1) * HALF], otf[f * HALF : (f + 1) * HALF]
        dr, di, orr, oi = d[:, :SUB], d[:, SUB:], o[:, :SUB], o[:, SUB:]
        parts.append((dr, di, orr, oi))
        terms = (dr * orr + di * oi, di * orr - dr * oi, orr * orr + oi * oi)
        if cross_real is None:
            cross_real, cross_imag, power = terms
        else:
            cross_real = cross_real + terms[0]
            cross_imag = cross_imag + terms[1]
            power = power + terms[2]
    inverse = 1.0 / (power + GAMMA)
    slope = weight * inverse
    xr, xi = cross_real * inverse, cross_imag * inverse
    share = weight * (xr * xr + xi * xi)
    cross_real, cross_imag = cross_real * slope, cross_imag * slope
    for dr, di, orr, oi in parts:
        bar_real = cross_real * dr + cross_imag * di - share * orr
        bar_imag = cross_real * di - cross_imag * dr - share * oi
        bars.append(jnp.concatenate([bar_real, bar_imag], 1))
    columns = right_mul(jnp.concatenate(bars, 0), tables["mixed"])
    yield
    evens, odds = [], []
    for f in range(FRAMES):
        part = columns[f * HALF : (f + 1) * HALF]
        evens.append(jnp.concatenate([part[:EVENS, :SUB], part[:EVENS, SUB:]], 0))
        odds.append(jnp.concatenate([part[EVENS:, :SUB], part[EVENS:, SUB:]], 0))
    even = left_mul(tables["even_t"], jnp.concatenate(evens, 1))
    odd = left_mul(tables["odd_t"], jnp.concatenate(odds, 1))
    yield
    psf_bar = fields_of(jnp.concatenate([even + odd, even - odd], 0))
    field_bar = jnp.concatenate(
        [field[:, (2 * f + part) * SUB : (2 * f + part + 1) * SUB] * psf_bar[f] for f in range(FRAMES) for part in (0, 1)],
        1,
    )
    half_bar = left_mul(tables["left_t"], field_bar)
    yield
    pieces = [half_bar[:, 2 * f * SUB : (2 * f + 2) * SUB] for f in range(FRAMES)]
    even_bar = right_mul_narrow(jnp.concatenate([p[:BAND] for p in pieces], 0), tables["right_even_t"])
    odd_bar = right_mul_narrow(jnp.concatenate([p[BAND:] for p in pieces], 0), tables["right_odd_t"])
    yield
    return [pupil * swap(bar) for pupil, bar in ((top, even_bar + odd_bar), (bottom, even_bar - odd_bar))]


MODE_ROWS = 48
MESH = pl.DeviceIdType.MESH


def plan(n, width, rows):
    team = n // TR
    share = n * 4 // TR // team
    strip = width * TR // (n * 4)
    first = [k * strip // SUB for k in range(share)]
    return team, share, strip, first, share * strip // SUB + 1


def mega_kernel(
    spots,
    n,
    width,
    rows,
    images_ref,
    anchors_hbm,
    patches_hbm,
    coeffs_hbm,
    zbasis_ref,
    fixed_hbm,
    pack_hbm,
    out_ref,
    anchors_ref,
    patches_ref,
    coeffs_ref,
    fixed_ref,
    tile_ref,
    everyone,
    owners,
    strips,
    pieces,
    zraw,
    zpad,
    ztable,
    pack_ref,
    phase_ref,
    total_ref,
    otf_ref,
    field_ref,
    pupil_ref,
    data_ref,
    current,
    wanted,
    mine_ref,
    slopes,
    local_sem,
    send_sem,
    recv_sem,
    strip_send,
    strip_recv,
    strip_local,
    hand_send,
    hand_recv,
):
    me = lax.axis_index("sub")
    team, share, strip, first, count = plan(n, width, rows)
    tile = me // team
    place = lax.rem(me, team)
    barrier = pltpu.get_barrier_semaphore()

    far = tile // 2
    planes = [3 - 3 * far, 2 - far, tile + 1 - 2 * lax.rem(tile, 2), tile]
    for plane in planes:

        def greet(step, carry, plane=plane):
            whom = plane * team + lax.rem(place + step, team)
            pl.semaphore_signal(barrier, inc=1, device_id=(whom,), device_id_type=MESH)
            return carry

        lax.fori_loop(1 if plane is tile else 0, team, greet, 0)

    load_anchors = pltpu.make_async_copy(anchors_hbm, anchors_ref, local_sem.at[2])
    load_patches = pltpu.make_async_copy(patches_hbm, patches_ref, local_sem.at[3])
    load_coeffs = pltpu.make_async_copy(coeffs_hbm, coeffs_ref, local_sem.at[4])
    load_fixed = pltpu.make_async_copy(fixed_hbm, fixed_ref, local_sem.at[5])
    load_basis = pltpu.make_async_copy(zbasis_ref, zraw, local_sem.at[0])
    load_pack = pltpu.make_async_copy(pack_hbm, pack_ref, local_sem.at[1])
    for load in (load_anchors, load_patches, load_coeffs, load_fixed, load_basis, load_pack):
        load.start()

    def source(whose, piece):
        at = jnp.minimum(whose * (share * strip) + piece * SUB, width - SUB)
        return images_ref.at[:, :, pl.ds(pl.multiple_of(at, SUB), SUB)]

    def landing(whose, piece):
        if rows % 8:
            return pieces.at[whose, :, :, pl.ds(piece * SUB, SUB)]
        return strips.at[:, pl.ds(pl.multiple_of(whose * rows, 8), rows), pl.ds(piece * SUB, SUB)]

    last = count - 1
    odd = lax.rem(place, 2) == 1
    reaches = odd & (place != team - 1)

    def own_copy(piece):
        return pltpu.make_async_copy(source(place, piece), landing(place, piece), strip_local.at[piece])

    for piece in range(last):
        own_copy(piece).start()

    @pl.when(reaches)
    def _():
        own_copy(last).start()

    load_anchors.wait()
    load_patches.wait()
    load_coeffs.wait()
    lane8 = lax.broadcasted_iota(jnp.int32, (8, SUB), 1)
    row8 = lax.broadcasted_iota(jnp.int32, (8, SUB), 0)
    message = jnp.zeros((8, SUB), F32)
    for t in range(TR):
        anchor = anchors_ref[t].astype(F32)
        patch = patches_ref[t].astype(F32)
        message = jnp.where((row8 == t) & (lane8 >= SLOT), anchor, message)
        message = jnp.where(row8 == TR + t, patch, message)
    tile_ref[...] = message
    modes = coeffs_ref.shape[2]
    for f in range(FRAMES):
        tile_ref[f : f + 1, :modes] = coeffs_ref[f]
    everyone[me] = tile_ref[...]

    pl.semaphore_wait(barrier, n - 1)

    def spread(block_ref, out_ref, stage, target):
        return pltpu.make_async_remote_copy(
            src_ref=block_ref,
            dst_ref=out_ref.at[me],
            send_sem=send_sem.at[stage],
            recv_sem=recv_sem.at[stage],
            device_id=(target,),
            device_id_type=MESH,
        )

    def begin_all(block_ref, out_ref, stage):
        for plane in planes:

            def begin(step, carry, plane=plane):
                spread(block_ref, out_ref, stage, plane * team + lax.rem(place + step, team)).start()
                return carry

            lax.fori_loop(1 if plane is tile else 0, team, begin, 0)

    def finish_all(out_ref, stage):
        part = out_ref.at[pl.ds(0, n - 1)]
        pltpu.make_async_copy(part, part, recv_sem.at[stage]).wait()

    begin_all(tile_ref, everyone, 0)

    def send_strip(piece, whose):
        return pltpu.make_async_remote_copy(
            src_ref=source(whose, piece),
            dst_ref=landing(place, piece),
            send_sem=strip_send.at[piece // last],
            recv_sem=strip_recv.at[piece],
            device_id=(tile * team + whose,),
            device_id_type=MESH,
        )

    for piece in range(last):

        def begin_strip(step, carry, piece=piece):
            send_strip(piece, lax.rem(place + step, team)).start()
            return carry

        lax.fori_loop(1, team, begin_strip, 0)

    def begin_last(i, carry):
        @pl.when(2 * i + 1 != place)
        def _():
            send_strip(last, 2 * i + 1).start()

        return carry

    lax.fori_loop(0, team // 2 - 1, begin_last, 0)

    def hand_on():
        return pltpu.make_async_remote_copy(
            src_ref=strips.at[:, :, pl.ds(0, SUB)],
            dst_ref=strips.at[:, :, pl.ds(last * SUB, SUB)],
            send_sem=hand_send.at[0],
            recv_sem=hand_recv.at[0],
            device_id=(me - 1,),
            device_id_type=MESH,
        )

    load_basis.wait()
    zpad[...] = jnp.zeros(zpad.shape, F32)
    zpad[:modes] = zraw[...]
    ztable[...] = jnp.zeros(ztable.shape, BF16)
    low48 = lax.broadcasted_iota(jnp.int32, (MODE_ROWS, SUB), 1) < PUP
    for i in range(0, BAND, 2):
        one, two = (zpad[:, c * SUB : (c + 1) * SUB] for c in (i // 2, BAND - 1 - i // 2))
        for j in range(2):
            basis_high, basis_low = split(jnp.where(low48, one, two))
            spot = slice((i + j) * SUB, (i + j + 1) * SUB)
            ztable[:MODE_ROWS, spot] = basis_high
            ztable[MODE_ROWS : 2 * MODE_ROWS, spot] = basis_low
            ztable[SUB : SUB + MODE_ROWS, spot] = basis_high
            one, two = swap(one), swap(two)

    finish_all(everyone, 0)

    low_rows, low_lanes = row8 < TR, lane8 < SLOT

    def patch_row(home, t):
        return everyone[home, pl.ds(TR + t, 1), :]

    def note_owner(device, carry):
        their_tile = device // team
        base = share * lax.rem(device, team)
        line = [patch_row(base + k, their_tile) for k in range(share)]
        owners[device] = jnp.where(
            low_rows, jnp.where(low_lanes, line[0], line[2]), jnp.where(low_lanes, line[1], line[3])
        )
        return carry

    def by_device(body, start):
        def block(i, carry):
            for j in range(8):
                carry = body(i * 8 + j, carry)
            return carry

        return lax.fori_loop(0, n // 8, block, start)

    by_device(note_owner, 0)
    for k in range(share):
        wanted[k] = jnp.broadcast_to(patch_row(share * place + k, tile), (8, SUB))
    wanted[share] = jnp.full((8, SUB), 1.0, F32) * me.astype(F32)

    def gather_coeffs(device, sums):
        block = everyone[device]
        number = device.astype(F32)
        return tuple(s + jnp.where(wanted[k] == number, block, 0.0) for k, s in enumerate(sums))

    zero8 = jnp.zeros((8, SUB), F32)
    found = by_device(gather_coeffs, (zero8,) * share)
    for k in range(share):
        current[k * FRAMES : (k + 1) * FRAMES, :] = jnp.where(low_lanes, found[k], 0.0)[:FRAMES]
    current[share * FRAMES : (share + 1) * FRAMES, :] = jnp.where(low_lanes, tile_ref[...], 0.0)[:FRAMES]

    load_pack.wait()
    load_fixed.wait()
    tables = Tables(pack_ref, spots)
    pixel_rows = PUP // 2
    chosen_rows = share * FRAMES

    def phases():
        value = current[:chosen_rows, :]
        lane = lax.broadcasted_iota(jnp.int32, value.shape, 1)
        high = value.astype(BF16).astype(F32)
        twice = jnp.where(lane < MODE_ROWS, high, pltpu.roll(high, MODE_ROWS, 1))
        left = jnp.concatenate([twice.astype(BF16), (value - high).astype(BF16)], 1)
        for c in range(0, pixel_rows, 2):
            phase = dot(left, ztable[:, c * SUB : (c + 2) * SUB])
            for half in range(2):
                for r in range(0, chosen_rows, 8):
                    phase_ref[pl.ds(r * pixel_rows + c + half, 8, stride=pixel_rows), :] = phase[
                        r : r + 8, half * SUB : (half + 1) * SUB
                    ]

    def window(k, c, lane, anchor, valid):
        shift = lax.rem(anchor, SUB)
        turn = lax.rem(SUB - shift, SUB)
        parts = []
        for cf in range(c * FRAMES, (c + 1) * FRAMES):
            at = first[k] * SUB
            one = pltpu.roll(strips[cf, :, pl.ds(at, SUB)], turn, 1)
            two = pltpu.roll(strips[cf, :, pl.ds(at + SUB, SUB)], turn, 1)
            cut = jnp.where(lane < SUB - shift, one, jnp.where(lane < valid, two, 0.0))
            parts.append(cut * fixed_ref[BAND + HALF :])
        return parts

    rows_of = [slice(c * FRAMES * HALF, (c + 1) * FRAMES * HALF) for c in range(CH)]
    lanes_of = [slice(2 * c * FRAMES * SUB, 2 * (c + 1) * FRAMES * SUB) for c in range(CH)]
    pixels_of = [slice(c * FRAMES * BAND, (c + 1) * FRAMES * BAND) for c in range(CH)]

    def spot(k):
        return pl.ds(k * SUB if isinstance(k, int) else pl.multiple_of(k * SUB, SUB), SUB)

    def forward(k, c):
        otf, field, top, bottom = yield from forward_channel(phase_ref[spot(k), :], c, fixed_ref, tables)
        otf_ref[k, rows_of[c], :] = otf
        field_ref[k, :, lanes_of[c]] = field
        pupil_ref[k, 0, pixels_of[c], :] = top
        pupil_ref[k, 1, pixels_of[c], :] = bottom

    def backward(k, c):
        return backward_channel(
            data_ref[k, rows_of[c], :],
            otf_ref[k, rows_of[c], :],
            field_ref[k, :, lanes_of[c]],
            pupil_ref[k, 0, pixels_of[c], :],
            pupil_ref[k, 1, pixels_of[c], :],
            fixed_ref,
            tables,
        )

    def forwards(*ks):
        return [forward(k, c) for k in ks for c in range(CH)]

    def backwards(*ks):
        return [backward(k, c) for k in ks for c in range(CH)]

    def keep_total(k, parts):
        total_ref[spot(k), :] = join_channels(parts)

    def wait_piece(piece):
        own_copy(piece).wait()
        if rows % 8:
            part = pieces.at[pl.ds(0, team - 1), :, :, pl.ds(piece * SUB, SUB)]
        else:
            part = strips.at[:, pl.ds(0, (team - 1) * rows), pl.ds(piece * SUB, SUB)]
        pltpu.make_async_copy(part, part, strip_recv.at[piece]).wait()
        if rows % 8:
            for q in range(team):
                strips[:, q * rows : (q + 1) * rows, piece * SUB : (piece + 1) * SUB] = pieces[
                    q, :, :, piece * SUB : (piece + 1) * SUB
                ]

    def wait_strip(piece):
        if piece == last:

            @pl.when(reaches)
            def _():
                wait_piece(last)

            @pl.when(jnp.logical_not(odd))
            def _():
                whole_strip = strips.at[:, :, pl.ds(last * SUB, SUB)]
                pltpu.make_async_copy(whole_strip, whole_strip, hand_recv.at[0]).wait()

        else:
            wait_piece(piece)
        if piece == 0:

            @pl.when(odd)
            def _():
                hand_on().start()

    lane128 = lax.broadcasted_iota(jnp.int32, (SUB, SUB), 1)

    def take_data(k, c):
        anchor = jnp.max(everyone[share * place + k, pl.ds(tile, 1), SLOT:]).astype(jnp.int32)
        begin = (place * share + k) * strip // SUB * SUB
        valid = jnp.where(begin + SUB <= width - SUB, SUB, 0)
        images = window(k, c, lane128, anchor, valid)
        data = yield from half_plane(images, tables, tables["data_mixed"])
        data_ref[k, rows_of[c], :] = data

    def data_then_backward(k, c):
        yield from take_data(k, c)
        yield
        return (yield from backward(k, c))

    def reduce_modes():
        block = jnp.concatenate(
            [total_ref[pl.ds(c, chosen_rows, stride=pixel_rows), :] for c in range(pixel_rows)], 1
        )
        both = jnp.concatenate(split(block), 0)
        result = lax.dot_general(
            both, ztable[:SUB], (((1,), (1,)), ((), ())), preferred_element_type=F32
        )
        high, low = result[:chosen_rows], result[chosen_rows:]
        lane = lax.broadcasted_iota(jnp.int32, high.shape, 1)
        slope = high + low + pltpu.roll(high, SUB - MODE_ROWS, 1)
        slope = jnp.where(lane < modes, slope, 0.0)
        return jnp.where(low_lanes, slope[:8], pltpu.roll(slope[8:], SLOT, 1))

    def fold(value):
        value = value + pltpu.roll(value, SLOT, 1)
        value = value + pltpu.roll(value, TR, 0)
        return jnp.where(low_lanes, value, 0.0)[:FRAMES]

    for iteration in range(ITERS):
        phases()
        if iteration == 0:

            def forward_body(i, carry):
                interleave(*forwards(2 * i, 2 * i + 1))
                return carry

            lax.fori_loop(0, share // 2, forward_body, 0)
            done = 0
            for k in range(share):
                while done <= first[k] + 1:
                    wait_strip(done)
                    done += 1
                keep_total(k, interleave(*[data_then_backward(k, c) for c in range(CH)]))
        else:
            interleave(*forwards(0, 1))
            for k in range(share - 2):
                keep_total(k, interleave(*backwards(k), *forwards(k + 2))[:CH])
            totals = interleave(*backwards(share - 2, share - 1))
            keep_total(share - 2, totals[:CH])
            keep_total(share - 1, totals[CH:])
        mine_ref[iteration] = reduce_modes()
        begin_all(mine_ref.at[iteration], slopes.at[iteration], 1 + iteration)
        slopes[iteration, me] = mine_ref[iteration]
        finish_all(slopes.at[iteration], 1 + iteration)

        needed = range(share if iteration == ITERS - 1 else 0, share + 1)
        def gather_slopes(device, sums, iteration=iteration):
            block = slopes[iteration, device]
            owner = owners[device]
            return tuple(s + jnp.where(owner == wanted[k], block, 0.0) for k, s in zip(needed, sums))

        sums = by_device(gather_slopes, (zero8,) * len(needed))
        for k in needed:
            gradient = fold(sums[k - needed[0]])
            at = k * FRAMES
            current[at : at + FRAMES, :] = current[at : at + FRAMES, :] - STEP_SIZE * gradient
            if k == share and iteration == ITERS - 1:
                fresh = current[at : at + FRAMES, :]
                for f in range(FRAMES):
                    out_ref[f] = fresh[f : f + 1, :modes]
                    out_ref[FRAMES + f] = gradient[f : f + 1, :modes]

    for stage, block in ((0, everyone), (1, slopes.at[0]), (2, slopes.at[1])):
        part = block.at[pl.ds(0, n - 1)]
        pltpu.make_async_copy(part, part, send_sem.at[stage]).wait()
    sent = images_ref.at[:, :, pl.ds(0, last * SUB)]
    for _ in range(team - 1):
        pltpu.make_async_copy(sent, sent, strip_send.at[0]).wait()

    def finish_last(i, carry):
        @pl.when(2 * i + 1 != place)
        def _():
            send_strip(last, 2 * i + 1).wait_send()

        return carry

    lax.fori_loop(0, team // 2 - 1, finish_last, 0)

    @pl.when(odd)
    def _():
        hand_on().wait_send()


def on_device(images, anchors, patches, coeffs, zbasis):
    n = lax.axis_size("sub")
    rows, width = images.shape[2:]
    modes = coeffs.shape[1]
    matrices, fixed = make_tables()
    pack, spots = pack_tables(matrices)
    pack, fixed = jnp.asarray(pack), jnp.asarray(fixed)
    team, share, strip, first, count = plan(n, width, rows)
    assert coeffs.shape[2] == 1 and anchors.shape[0] == 4 and share == 4
    pixels = zbasis.shape[1]
    piece_shape = (team, FIELDS, rows, count * SUB) if rows % 8 else (1, 1, 8, SUB)
    out_shape = jax.ShapeDtypeStruct((2 * FRAMES, 1, modes), F32)
    anywhere = pl.BlockSpec(memory_space=pl.ANY)
    vmem = pl.BlockSpec(memory_space=pltpu.VMEM)
    both = pl.pallas_call(
        functools.partial(mega_kernel, spots, n, width, rows),
        out_shape=out_shape,
        in_specs=[anywhere] * 7,
        out_specs=vmem,
        scratch_shapes=[
            pltpu.SMEM(anchors.shape, jnp.int32),
            pltpu.SMEM(patches.shape, jnp.int32),
            pltpu.VMEM((FRAMES, 1, modes), F32),
            pltpu.VMEM(fixed.shape, F32),
            pltpu.VMEM((8, SUB), F32),
            pltpu.VMEM((n, 8, SUB), F32),
            pltpu.VMEM((n, 8, SUB), F32),
            pltpu.VMEM((FIELDS, SUB, count * SUB), F32),
            pltpu.VMEM(piece_shape, F32),
            pltpu.VMEM((modes, pixels), F32),
            pltpu.VMEM((MODE_ROWS, pixels), F32),
            pltpu.VMEM((2 * SUB, pixels), BF16),
            pltpu.VMEM(pack.shape, BF16),
            pltpu.VMEM((share * SUB, SUB), F32),
            pltpu.VMEM((share * SUB, SUB), F32),
            pltpu.VMEM((share, FIELDS * HALF, 2 * SUB), F32),
            pltpu.VMEM((share, SUB, 2 * FIELDS * SUB), F32),
            pltpu.VMEM((share, 2, FIELDS * BAND, SUB), F32),
            pltpu.VMEM((share, FIELDS * HALF, 2 * SUB), F32),
            pltpu.VMEM(((share + 1) * FRAMES + 4, SUB), F32),
            pltpu.VMEM((share + 1, 8, SUB), F32),
            pltpu.VMEM((ITERS, 8, SUB), F32),
            pltpu.VMEM((ITERS, n, 8, SUB), F32),
            pltpu.SemaphoreType.DMA((6,)),
            pltpu.SemaphoreType.DMA((1 + ITERS,)),
            pltpu.SemaphoreType.DMA((1 + ITERS,)),
            pltpu.SemaphoreType.DMA((2,)),
            pltpu.SemaphoreType.DMA((count,)),
            pltpu.SemaphoreType.DMA((count,)),
            pltpu.SemaphoreType.DMA((1,)),
            pltpu.SemaphoreType.DMA((1,)),
        ],
        compiler_params=pltpu.CompilerParams(
            collective_id=0, has_side_effects=True, vmem_limit_bytes=VMEM_LIMIT
        ),
    )(
        images.reshape(FIELDS, rows, width),
        anchors,
        patches,
        coeffs.transpose(0, 2, 1),
        zbasis,
        fixed,
        pack,
    )
    both = both.transpose(0, 2, 1)
    return both[:FRAMES], both[FRAMES:]


def solution(mesh):
    return jax.shard_map(
        on_device,
        mesh=mesh,
        in_specs=(P(None, None, "sub", None), P("sub"), P("sub"), P(None, None, "sub"), P()),
        out_specs=(P(None, None, "sub"), P(None, None, "sub")),
        check_vma=False,
    )
```

```python
import functools
import math

import jax
import jax.numpy as jnp
import ml_dtypes
import numpy as np
from jax import lax
from jax.experimental import pallas as pl
from jax.experimental.pallas import tpu as pltpu
from jax.sharding import PartitionSpec as P

SUB = 128
CH = 2
FRAMES = 4
FIELDS = CH * FRAMES
SLOT = 64
TR = 4
ITERS = 2
PUP = 64
HALF = 72
EVENS = 40
BAND = 32
GAMMA = 0.01
STEP_SIZE = 0.05
F32 = jnp.float32
BF16 = jnp.bfloat16
VMEM_LIMIT = 60 << 20
SIN = (-1.6666666e-1, 8.3333310e-3, -1.9840874e-4, 2.7525562e-6, -2.3889859e-8)
COS = (-0.5, 4.1666666e-2, -1.3888889e-3, 2.4801587e-5, -2.7557319e-7, 2.0876757e-9)


def split_np(matrix):
    matrix = np.asarray(matrix, np.float32)
    high = matrix.astype(ml_dtypes.bfloat16)
    low = (matrix - high.astype(np.float32)).astype(ml_dtypes.bfloat16)
    return high, low


def cos_sin(rows, columns):
    angle = 2.0 * np.pi * np.outer(rows, columns) / SUB
    return np.cos(angle), np.sin(angle)


def make_tables():
    k = np.arange(SUB)
    cos, sin = cos_sin(k, k)
    taper = 0.5 - 0.5 * np.cos(2.0 * np.pi * (k + 0.5) / SUB)
    centred = np.arange(PUP) - PUP / 2 + 0.5
    mask = (centred[:, None] ** 2 + centred[None, :] ** 2 <= (PUP / 2) ** 2).astype(np.float32)
    scale = 1.0 / (SUB * SUB * float(mask.sum()))
    c, s = cos[:PUP], sin[:PUP]
    right_even = np.block([[c, -s], [s, c]])
    right_odd = np.block([[-s, -c], [c, -s]])
    left = np.concatenate(cos_sin(k, centred[:BAND]), 1)
    even, odd = np.zeros((2 * EVENS, PUP)), np.zeros((PUP, PUP))
    even[:33], even[EVENS : EVENS + 33] = cos_sin(np.arange(0, 65, 2), np.arange(PUP))
    odd[:BAND], odd[BAND:] = cos_sin(np.arange(1, 64, 2), np.arange(PUP))
    mixed = np.block([[cos, -sin], [-sin, -cos]])
    weight = np.zeros((HALF, 1))
    weight[:33] = weight[EVENS:] = 2.0
    weight[0] = weight[32] = 1.0
    weight = np.broadcast_to(weight * (-2.0 / SUB**4), (HALF, SUB))
    rows_taper = np.broadcast_to(taper[:, None] / scale, (SUB, SUB))
    packed_mask = np.concatenate([mask[:BAND], mask[::-1][:BAND]], 1)
    fixed = np.concatenate([packed_mask, weight, rows_taper], 0).astype(np.float32)
    matrices = {
        "right_even": (right_even, "down"),
        "right_odd": (right_odd, "down"),
        "left": (left, "across"),
        "even": (even * scale, "across"),
        "odd": (odd * scale, "across"),
        "mixed": (mixed, "down"),
        "data_mixed": (np.concatenate([taper, taper])[:, None] * mixed, "down"),
        "even_t": (even.T * (2.0 * scale), "across"),
        "odd_t": (odd.T * (2.0 * scale), "across"),
        "left_t": (left.T, "across"),
        "right_even_t": (right_even.T, "square"),
        "right_odd_t": (right_odd.T, "square"),
    }
    return matrices, fixed


def pack_tables(matrices):
    spots, parts, at = {}, [], 0
    width = 3 * SUB
    for name, (matrix, form) in matrices.items():
        high, low = split_np(matrix)
        if form == "square":
            part = np.block([[high, low], [high, np.zeros_like(low)]])
        else:
            part = np.concatenate([high, high, low], 0 if form == "down" else 1)
        spots[name] = (at, part.shape[0], part.shape[1])
        parts.append(np.pad(part, ((0, -part.shape[0] % 16), (0, width - part.shape[1]))))
        at += parts[-1].shape[0]
    return np.concatenate(parts, 0), spots


class Tables:
    def __init__(self, ref, spots):
        self.ref, self.spots = ref, spots

    def __getitem__(self, name):
        at, height, width = self.spots[name]
        return self.ref[at : at + height, :width]


def split(value):
    high = value.astype(BF16)
    low = (value - high.astype(F32)).astype(BF16)
    return high, low


def dot(a, b):
    return jnp.dot(a, b, preferred_element_type=F32)


def left_mul(table, value):
    high, low = split(value)
    return dot(table, jnp.concatenate([high, low, high], 0))


def right_mul(value, table):
    high, low = split(value)
    return dot(jnp.concatenate([high, low, high], 1), table)


def right_mul_narrow(value, table):
    both = dot(jnp.concatenate(split(value), 1), table)
    return both[:, :SUB] + both[:, SUB:]


def channel_waves(angle, mask):
    turns = jnp.floor(angle * np.float32(1.0 / math.pi) + 0.5)
    rest = angle - turns * np.float32(3.140625)
    rest = rest - turns * np.float32(9.67025756835937500e-4)
    rest = rest - turns * np.float32(6.2771141529083252e-7)
    square = rest * rest
    sine = SIN[-1]
    for term in SIN[-2::-1]:
        sine = sine * square + term
    sine = rest + rest * (square * sine)
    cosine = COS[-1]
    for term in COS[-2::-1]:
        cosine = cosine * square + term
    cosine = 1.0 + square * cosine
    sine2, cosine2 = (sine + sine) * cosine, 1.0 - (sine + sine) * sine
    double = (sine2 + sine2) * mask
    sine4, cosine4 = double * cosine2, mask - double * sine2
    sign = 1.0 - 2.0 * (turns - 2.0 * jnp.floor(turns * 0.5))
    sine, cosine = sine * sign, cosine * sign
    return (cosine * cosine4 - sine * sine4, sine * cosine4 + cosine * sine4), (cosine4, sine4)


def fields_of(value):
    return [value[:, at : at + SUB] for at in range(0, value.shape[1], SUB)]


def interleave(*chains):
    results, live = [None] * len(chains), list(enumerate(chains))
    while live:
        still = []
        for at, chain in live:
            try:
                next(chain)
                still.append((at, chain))
            except StopIteration as stop:
                results[at] = stop.value
        live = still
    return results


def half_plane(images, tables, mixed):
    upper = jnp.concatenate([image[:PUP] + image[PUP:] for image in images], 1)
    lower = jnp.concatenate([image[:PUP] - image[PUP:] for image in images], 1)
    evens = left_mul(tables["even"], upper)
    odds = left_mul(tables["odd"], lower)
    stacked = [
        jnp.concatenate(
            [
                jnp.concatenate([even[:EVENS], odd[:BAND]], 0),
                jnp.concatenate([even[EVENS:], odd[BAND:]], 0),
            ],
            1,
        )
        for even, odd in zip(fields_of(evens), fields_of(odds))
    ]
    yield
    return right_mul(jnp.concatenate(stacked, 0), mixed)


def swap(value):
    return pltpu.roll(value, PUP, 1)


def forward_channel(waves, tables):
    cosine, sine = waves
    low = lax.broadcasted_iota(jnp.int32, cosine.shape, 1) < PUP
    top = jnp.where(low, cosine, swap(sine))
    bottom = jnp.where(low, swap(cosine), sine)
    even = right_mul(top + bottom, tables["right_even"])
    odd = right_mul(top - bottom, tables["right_odd"])
    yield
    blocks = jnp.concatenate(
        [
            jnp.concatenate([part[f * BAND : (f + 1) * BAND] for part in (even, odd)], 0)
            for f in range(FRAMES)
        ],
        1,
    )
    field = left_mul(tables["left"], blocks)
    yield
    images = []
    for f in range(FRAMES):
        real = field[:, 2 * f * SUB : (2 * f + 1) * SUB]
        imag = field[:, (2 * f + 1) * SUB : (2 * f + 2) * SUB]
        images.append(real * real + imag * imag)
    otf = yield from half_plane(images, tables, tables["mixed"])
    yield
    return otf, field, top, bottom


def join_channels(parts):
    sums = parts[0]
    for c in range(1, CH):
        ratio = np.float32(1.0 / (1.0 + 0.25 * c))
        sums = [a + b * ratio for a, b in zip(sums, parts[c])]
    low = lax.broadcasted_iota(jnp.int32, sums[0].shape, 1) < PUP
    return jnp.where(low, sums[0] - swap(sums[0]), swap(sums[1]) - sums[1])


def backward_channel(data, otf, field, top, bottom, fixed_ref, tables):
    weight = fixed_ref[BAND : BAND + HALF]
    parts, bars = [], []
    cross_real = cross_imag = power = None
    for f in range(FRAMES):
        d, o = data[f * HALF : (f + 1) * HALF], otf[f * HALF : (f + 1) * HALF]
        dr, di, orr, oi = d[:, :SUB], d[:, SUB:], o[:, :SUB], o[:, SUB:]
        parts.append((dr, di, orr, oi))
        terms = (dr * orr + di * oi, di * orr - dr * oi, orr * orr + oi * oi)
        if cross_real is None:
            cross_real, cross_imag, power = terms
        else:
            cross_real = cross_real + terms[0]
            cross_imag = cross_imag + terms[1]
            power = power + terms[2]
    inverse = 1.0 / (power + GAMMA)
    slope = weight * inverse
    xr, xi = cross_real * inverse, cross_imag * inverse
    share = weight * (xr * xr + xi * xi)
    cross_real, cross_imag = cross_real * slope, cross_imag * slope
    for dr, di, orr, oi in parts:
        bar_real = cross_real * dr + cross_imag * di - share * orr
        bar_imag = cross_real * di - cross_imag * dr - share * oi
        bars.append(jnp.concatenate([bar_real, bar_imag], 1))
    columns = right_mul(jnp.concatenate(bars, 0), tables["mixed"])
    yield
    evens, odds = [], []
    for f in range(FRAMES):
        part = columns[f * HALF : (f + 1) * HALF]
        evens.append(jnp.concatenate([part[:EVENS, :SUB], part[:EVENS, SUB:]], 0))
        odds.append(jnp.concatenate([part[EVENS:, :SUB], part[EVENS:, SUB:]], 0))
    even = left_mul(tables["even_t"], jnp.concatenate(evens, 1))
    odd = left_mul(tables["odd_t"], jnp.concatenate(odds, 1))
    yield
    psf_bar = fields_of(jnp.concatenate([even + odd, even - odd], 0))
    field_bar = jnp.concatenate(
        [field[:, (2 * f + part) * SUB : (2 * f + part + 1) * SUB] * psf_bar[f] for f in range(FRAMES) for part in (0, 1)],
        1,
    )
    half_bar = left_mul(tables["left_t"], field_bar)
    yield
    pieces = [half_bar[:, 2 * f * SUB : (2 * f + 2) * SUB] for f in range(FRAMES)]
    even_bar = right_mul_narrow(jnp.concatenate([p[:BAND] for p in pieces], 0), tables["right_even_t"])
    odd_bar = right_mul_narrow(jnp.concatenate([p[BAND:] for p in pieces], 0), tables["right_odd_t"])
    yield
    return [pupil * swap(bar) for pupil, bar in ((top, even_bar + odd_bar), (bottom, even_bar - odd_bar))]


MODE_ROWS = 48
PACKED = 6
CHUNK = 16
MESH = pl.DeviceIdType.MESH


def plan(n, width, rows):
    team = n // TR
    share = n * 4 // TR // team
    strip = width * TR // (n * 4)
    first = [k * strip // SUB for k in range(share)]
    return team, share, strip, first, share * strip // SUB + 1


def mega_kernel(
    spots,
    n,
    width,
    rows,
    images_ref,
    anchors_hbm,
    patches_hbm,
    coeffs_hbm,
    zbasis_ref,
    fixed_hbm,
    pack_hbm,
    out_ref,
    anchors_ref,
    patches_ref,
    coeffs_ref,
    fixed_ref,
    tile_ref,
    everyone,
    owners,
    strips,
    pieces,
    zraw,
    zpad,
    ztable,
    pack_ref,
    phase_ref,
    total_ref,
    otf_ref,
    field_ref,
    pupil_ref,
    data_ref,
    current,
    wanted,
    mine_ref,
    slopes,
    unpack_ref,
    local_sem,
    send_sem,
    recv_sem,
    strip_send,
    strip_recv,
    strip_local,
    hand_send,
    hand_recv,
):
    me = lax.axis_index("sub")
    team, share, strip, first, count = plan(n, width, rows)
    tile = me // team
    place = lax.rem(me, team)
    barrier = pltpu.get_barrier_semaphore()

    far = tile // 2
    planes = [3 - 3 * far, 2 - far, tile + 1 - 2 * lax.rem(tile, 2), tile]
    for plane in planes:

        def greet(step, carry, plane=plane):
            whom = plane * team + lax.rem(place + step, team)
            pl.semaphore_signal(barrier, inc=1, device_id=(whom,), device_id_type=MESH)
            return carry

        lax.fori_loop(1 if plane is tile else 0, team, greet, 0)

    load_anchors = pltpu.make_async_copy(anchors_hbm, anchors_ref, local_sem.at[2])
    load_patches = pltpu.make_async_copy(patches_hbm, patches_ref, local_sem.at[3])
    load_coeffs = pltpu.make_async_copy(coeffs_hbm, coeffs_ref, local_sem.at[4])
    load_fixed = pltpu.make_async_copy(fixed_hbm, fixed_ref, local_sem.at[5])
    load_basis = pltpu.make_async_copy(zbasis_ref, zraw, local_sem.at[0])
    load_pack = pltpu.make_async_copy(pack_hbm, pack_ref, local_sem.at[1])
    for load in (load_anchors, load_patches, load_coeffs, load_fixed, load_basis, load_pack):
        load.start()

    def source(whose, piece):
        at = jnp.minimum(whose * (share * strip) + piece * SUB, width - SUB)
        return images_ref.at[:, :, pl.ds(pl.multiple_of(at, SUB), SUB)]

    def landing(whose, piece):
        if rows % 8:
            return pieces.at[whose, :, :, pl.ds(piece * SUB, SUB)]
        return strips.at[:, pl.ds(pl.multiple_of(whose * rows, 8), rows), pl.ds(piece * SUB, SUB)]

    last = count - 1
    odd = lax.rem(place, 2) == 1
    reaches = odd & (place != team - 1)

    def own_copy(piece):
        return pltpu.make_async_copy(source(place, piece), landing(place, piece), strip_local.at[piece])

    for piece in range(last):
        own_copy(piece).start()

    @pl.when(reaches)
    def _():
        own_copy(last).start()

    load_anchors.wait()
    load_patches.wait()
    load_coeffs.wait()
    lane8 = lax.broadcasted_iota(jnp.int32, (8, SUB), 1)
    row8 = lax.broadcasted_iota(jnp.int32, (8, SUB), 0)
    message = jnp.zeros((8, SUB), F32)
    for t in range(TR):
        anchor = anchors_ref[t].astype(F32)
        patch = patches_ref[t].astype(F32)
        message = jnp.where((row8 == t) & (lane8 >= SLOT), anchor, message)
        message = jnp.where(row8 == TR + t, patch, message)
    tile_ref[...] = message
    modes = coeffs_ref.shape[2]
    for f in range(FRAMES):
        tile_ref[f : f + 1, :modes] = coeffs_ref[f]
    everyone[me] = tile_ref[...]

    pl.semaphore_wait(barrier, n - 1)

    def spread(block_ref, out_ref, stage, target):
        return pltpu.make_async_remote_copy(
            src_ref=block_ref,
            dst_ref=out_ref.at[me],
            send_sem=send_sem.at[stage],
            recv_sem=recv_sem.at[stage],
            device_id=(target,),
            device_id_type=MESH,
        )

    def begin_all(block_ref, out_ref, stage):
        for plane in planes:

            def begin(step, carry, plane=plane):
                spread(block_ref, out_ref, stage, plane * team + lax.rem(place + step, team)).start()
                return carry

            lax.fori_loop(1 if plane is tile else 0, team, begin, 0)

    def finish_all(out_ref, stage):
        part = out_ref.at[pl.ds(0, n - 1)]
        pltpu.make_async_copy(part, part, recv_sem.at[stage]).wait()

    begin_all(tile_ref, everyone, 0)

    def send_strip(piece, whose):
        return pltpu.make_async_remote_copy(
            src_ref=source(whose, piece),
            dst_ref=landing(place, piece),
            send_sem=strip_send.at[piece // last],
            recv_sem=strip_recv.at[piece],
            device_id=(tile * team + whose,),
            device_id_type=MESH,
        )

    for piece in range(last):

        def begin_strip(step, carry, piece=piece):
            send_strip(piece, lax.rem(place + step, team)).start()
            return carry

        lax.fori_loop(1, team, begin_strip, 0)

    def begin_last(i, carry):
        @pl.when(2 * i + 1 != place)
        def _():
            send_strip(last, 2 * i + 1).start()

        return carry

    lax.fori_loop(0, team // 2 - 1, begin_last, 0)

    def hand_on():
        return pltpu.make_async_remote_copy(
            src_ref=strips.at[:, :, pl.ds(0, SUB)],
            dst_ref=strips.at[:, :, pl.ds(last * SUB, SUB)],
            send_sem=hand_send.at[0],
            recv_sem=hand_recv.at[0],
            device_id=(me - 1,),
            device_id_type=MESH,
        )

    load_basis.wait()
    zpad[...] = jnp.zeros(zpad.shape, F32)
    zpad[:modes] = zraw[...]
    ztable[...] = jnp.zeros(ztable.shape, BF16)
    low48 = lax.broadcasted_iota(jnp.int32, (MODE_ROWS, SUB), 1) < PUP
    for i in range(0, BAND, 2):
        one, two = (zpad[:, c * SUB : (c + 1) * SUB] for c in (i // 2, BAND - 1 - i // 2))
        for j in range(2):
            basis_high, basis_low = split(jnp.where(low48, one, two))
            spot = slice((i + j) * SUB, (i + j + 1) * SUB)
            ztable[:MODE_ROWS, spot] = basis_high
            ztable[MODE_ROWS : 2 * MODE_ROWS, spot] = basis_low
            ztable[SUB : SUB + MODE_ROWS, spot] = basis_high
            one, two = swap(one), swap(two)

    finish_all(everyone, 0)

    low_lanes = lane8 < SLOT
    lane6 = lax.broadcasted_iota(jnp.int32, (PACKED, SUB), 1)
    row6 = lax.broadcasted_iota(jnp.int32, (PACKED, SUB), 0)

    def patch_row(home, t):
        return everyone[home, pl.ds(TR + t, 1), :]

    def note_owner(device, carry):
        their_tile = device // team
        base = share * lax.rem(device, team)
        line = [patch_row(base + k, their_tile) for k in range(share)]
        owner = jnp.where(
            row6 < TR,
            jnp.where(lane6 < MODE_ROWS, line[0], line[2]),
            jnp.where(lane6 < MODE_ROWS, line[1], line[3]),
        )
        extra = jnp.where(row6 < PACKED // 2, line[1], line[3])
        owners[device] = jnp.where(lane6 < 2 * MODE_ROWS, owner, extra)
        return carry

    def by_device(body, start):
        def block(i, carry):
            for j in range(8):
                carry = body(i * 8 + j, carry)
            return carry

        return lax.fori_loop(0, n // 8, block, start)

    by_device(note_owner, 0)
    for k in range(share):
        wanted[k] = jnp.broadcast_to(patch_row(share * place + k, tile), (8, SUB))
    wanted[share] = jnp.full((8, SUB), 1.0, F32) * me.astype(F32)

    def gather_coeffs(device, sums):
        block = everyone[device]
        number = device.astype(F32)
        return tuple(s + jnp.where(wanted[k] == number, block, 0.0) for k, s in enumerate(sums))

    zero8 = jnp.zeros((8, SUB), F32)
    found = by_device(gather_coeffs, (zero8,) * share)
    for k in range(share):
        current[k * FRAMES : (k + 1) * FRAMES, :] = jnp.where(low_lanes, found[k], 0.0)[:FRAMES]
    current[share * FRAMES : (share + 1) * FRAMES, :] = jnp.where(low_lanes, tile_ref[...], 0.0)[:FRAMES]

    load_pack.wait()
    load_fixed.wait()
    tables = Tables(pack_ref, spots)
    pixel_rows = PUP // 2
    chosen_rows = share * FRAMES

    def phases():
        value = current[:chosen_rows, :]
        lane = lax.broadcasted_iota(jnp.int32, value.shape, 1)
        high = value.astype(BF16).astype(F32)
        twice = jnp.where(lane < MODE_ROWS, high, pltpu.roll(high, MODE_ROWS, 1))
        left = jnp.concatenate([twice.astype(BF16), (value - high).astype(BF16)], 1)
        for c in range(0, pixel_rows, 2):
            phase = dot(left, ztable[:, c * SUB : (c + 2) * SUB])
            for half in range(2):
                for r in range(0, chosen_rows, 8):
                    phase_ref[pl.ds(r * pixel_rows + c + half, 8, stride=pixel_rows), :] = phase[
                        r : r + 8, half * SUB : (half + 1) * SUB
                    ]

    def window(k, c, lane, anchor, valid):
        shift = lax.rem(anchor, SUB)
        turn = lax.rem(SUB - shift, SUB)
        parts = []
        for cf in range(c * FRAMES, (c + 1) * FRAMES):
            at = first[k] * SUB
            one = pltpu.roll(strips[cf, :, pl.ds(at, SUB)], turn, 1)
            two = pltpu.roll(strips[cf, :, pl.ds(at + SUB, SUB)], turn, 1)
            cut = jnp.where(lane < SUB - shift, one, jnp.where(lane < valid, two, 0.0))
            parts.append(cut * fixed_ref[BAND + HALF :])
        return parts

    rows_of = [slice(c * FRAMES * HALF, (c + 1) * FRAMES * HALF) for c in range(CH)]
    lanes_of = [slice(2 * c * FRAMES * SUB, 2 * (c + 1) * FRAMES * SUB) for c in range(CH)]
    pixels_of = [slice(c * FRAMES * BAND, (c + 1) * FRAMES * BAND) for c in range(CH)]

    def spot(k):
        return pl.ds(k * SUB if isinstance(k, int) else pl.multiple_of(k * SUB, SUB), SUB)

    def forward(k, c, waves):
        if not waves:
            mask = jnp.concatenate([fixed_ref[:BAND]] * FRAMES, 0)
            waves += channel_waves(phase_ref[spot(k), :] * np.float32(0.2), mask)
        otf, field, top, bottom = yield from forward_channel(waves[c], tables)
        otf_ref[k, rows_of[c], :] = otf
        field_ref[k, :, lanes_of[c]] = field
        pupil_ref[k, 0, pixels_of[c], :] = top
        pupil_ref[k, 1, pixels_of[c], :] = bottom

    def backward(k, c):
        return backward_channel(
            data_ref[k, rows_of[c], :],
            otf_ref[k, rows_of[c], :],
            field_ref[k, :, lanes_of[c]],
            pupil_ref[k, 0, pixels_of[c], :],
            pupil_ref[k, 1, pixels_of[c], :],
            fixed_ref,
            tables,
        )

    def forwards(*ks):
        shared = {k: [] for k in range(len(ks))}
        return [forward(k, c, shared[i]) for i, k in enumerate(ks) for c in range(CH)]

    def backwards(*ks):
        return [backward(k, c) for k in ks for c in range(CH)]

    def keep_total(k, parts):
        total_ref[spot(k), :] = join_channels(parts)

    def wait_piece(piece):
        own_copy(piece).wait()
        if rows % 8:
            part = pieces.at[pl.ds(0, team - 1), :, :, pl.ds(piece * SUB, SUB)]
        else:
            part = strips.at[:, pl.ds(0, (team - 1) * rows), pl.ds(piece * SUB, SUB)]
        pltpu.make_async_copy(part, part, strip_recv.at[piece]).wait()
        if rows % 8:
            for q in range(team):
                strips[:, q * rows : (q + 1) * rows, piece * SUB : (piece + 1) * SUB] = pieces[
                    q, :, :, piece * SUB : (piece + 1) * SUB
                ]

    def wait_strip(piece):
        if piece == last:

            @pl.when(reaches)
            def _():
                wait_piece(last)

            @pl.when(jnp.logical_not(odd))
            def _():
                whole_strip = strips.at[:, :, pl.ds(last * SUB, SUB)]
                pltpu.make_async_copy(whole_strip, whole_strip, hand_recv.at[0]).wait()

        else:
            wait_piece(piece)
        if piece == 0:

            @pl.when(odd)
            def _():
                hand_on().start()

    lane128 = lax.broadcasted_iota(jnp.int32, (SUB, SUB), 1)

    def take_data(k, c):
        anchor = jnp.max(everyone[share * place + k, pl.ds(tile, 1), SLOT:]).astype(jnp.int32)
        begin = (place * share + k) * strip // SUB * SUB
        valid = jnp.where(begin + SUB <= width - SUB, SUB, 0)
        images = window(k, c, lane128, anchor, valid)
        data = yield from half_plane(images, tables, tables["data_mixed"])
        data_ref[k, rows_of[c], :] = data

    def data_then_backward(k, c):
        yield from take_data(k, c)
        yield
        return (yield from backward(k, c))

    def reduce_modes():
        block = jnp.concatenate(
            [total_ref[pl.ds(c, chosen_rows, stride=pixel_rows), :] for c in range(pixel_rows)], 1
        )
        both = jnp.concatenate(split(block), 0)
        result = lax.dot_general(
            both, ztable[:SUB], (((1,), (1,)), ((), ())), preferred_element_type=F32
        )
        high, low = result[:chosen_rows], result[chosen_rows:]
        lane = lax.broadcasted_iota(jnp.int32, high.shape, 1)
        slope = high + low + pltpu.roll(high, SUB - MODE_ROWS, 1)
        slope = jnp.where(lane < modes, slope, 0.0)
        wide = slope[:8] + pltpu.roll(slope[8:], MODE_ROWS, 1)
        packed = jnp.where(lane8 < 2 * MODE_ROWS, wide, 0.0)
        for j in range(PACKED):
            for extra in range(2):
                at = 2 * MODE_ROWS + extra * CHUNK
                line = jnp.broadcast_to(wide[PACKED + extra : PACKED + extra + 1], (8, SUB))
                here = (row8 == j) & (lane8 >= at) & (lane8 < at + CHUNK)
                packed = jnp.where(here, pltpu.roll(line, at - CHUNK * j, 1), packed)
        return packed[:PACKED]

    def fold(packed):
        unpack_ref[:PACKED] = packed
        value = unpack_ref[...]
        whole = jnp.where((row8 < PACKED) & (lane8 < 2 * MODE_ROWS), value, 0.0)
        for j in range(PACKED):
            line = jnp.broadcast_to(value[j : j + 1], (8, SUB))
            for extra in range(2):
                here = (row8 == PACKED + extra) & (lane8 >= CHUNK * j) & (lane8 < CHUNK * (j + 1))
                at = 2 * MODE_ROWS + extra * CHUNK
                whole = jnp.where(here, pltpu.roll(line, SUB + CHUNK * j - at, 1), whole)
        whole = whole + pltpu.roll(whole, SUB - MODE_ROWS, 1)
        whole = whole + pltpu.roll(whole, TR, 0)
        return jnp.where(lane8 < MODE_ROWS, whole, 0.0)[:FRAMES]

    for iteration in range(ITERS):
        phases()
        if iteration == 0:

            def forward_body(i, carry):
                interleave(*forwards(2 * i, 2 * i + 1))
                return carry

            lax.fori_loop(0, share // 2, forward_body, 0)
            done = 0
            for k in range(share):
                while done <= first[k] + 1:
                    wait_strip(done)
                    done += 1
                keep_total(k, interleave(*[data_then_backward(k, c) for c in range(CH)]))
        else:
            interleave(*forwards(0, 1))
            for k in range(share - 2):
                keep_total(k, interleave(*backwards(k), *forwards(k + 2))[:CH])
            totals = interleave(*backwards(share - 2, share - 1))
            keep_total(share - 2, totals[:CH])
            keep_total(share - 1, totals[CH:])
        mine_ref[iteration] = reduce_modes()
        begin_all(mine_ref.at[iteration], slopes.at[iteration], 1 + iteration)
        slopes[iteration, me] = mine_ref[iteration]
        finish_all(slopes.at[iteration], 1 + iteration)

        needed = range(share if iteration == ITERS - 1 else 0, share + 1)
        def gather_slopes(device, sums, iteration=iteration):
            block = slopes[iteration, device]
            owner = owners[device]
            return tuple(s + jnp.where(owner == wanted[k, :PACKED], block, 0.0) for k, s in zip(needed, sums))

        sums = by_device(gather_slopes, (jnp.zeros((PACKED, SUB), F32),) * len(needed))
        for k in needed:
            gradient = fold(sums[k - needed[0]])
            at = k * FRAMES
            current[at : at + FRAMES, :] = current[at : at + FRAMES, :] - STEP_SIZE * gradient
            if k == share and iteration == ITERS - 1:
                fresh = current[at : at + FRAMES, :]
                for f in range(FRAMES):
                    out_ref[f] = fresh[f : f + 1, :modes]
                    out_ref[FRAMES + f] = gradient[f : f + 1, :modes]

    for stage, block in ((0, everyone), (1, slopes.at[0]), (2, slopes.at[1])):
        part = block.at[pl.ds(0, n - 1)]
        pltpu.make_async_copy(part, part, send_sem.at[stage]).wait()
    sent = images_ref.at[:, :, pl.ds(0, last * SUB)]
    for _ in range(team - 1):
        pltpu.make_async_copy(sent, sent, strip_send.at[0]).wait()

    def finish_last(i, carry):
        @pl.when(2 * i + 1 != place)
        def _():
            send_strip(last, 2 * i + 1).wait_send()

        return carry

    lax.fori_loop(0, team // 2 - 1, finish_last, 0)

    @pl.when(odd)
    def _():
        hand_on().wait_send()


def on_device(images, anchors, patches, coeffs, zbasis):
    n = lax.axis_size("sub")
    rows, width = images.shape[2:]
    modes = coeffs.shape[1]
    matrices, fixed = make_tables()
    pack, spots = pack_tables(matrices)
    pack, fixed = jnp.asarray(pack), jnp.asarray(fixed)
    team, share, strip, first, count = plan(n, width, rows)
    assert coeffs.shape[2] == 1 and anchors.shape[0] == 4 and share == 4
    pixels = zbasis.shape[1]
    piece_shape = (team, FIELDS, rows, count * SUB) if rows % 8 else (1, 1, 8, SUB)
    out_shape = jax.ShapeDtypeStruct((2 * FRAMES, 1, modes), F32)
    anywhere = pl.BlockSpec(memory_space=pl.ANY)
    vmem = pl.BlockSpec(memory_space=pltpu.VMEM)
    both = pl.pallas_call(
        functools.partial(mega_kernel, spots, n, width, rows),
        out_shape=out_shape,
        in_specs=[anywhere] * 7,
        out_specs=vmem,
        scratch_shapes=[
            pltpu.SMEM(anchors.shape, jnp.int32),
            pltpu.SMEM(patches.shape, jnp.int32),
            pltpu.VMEM((FRAMES, 1, modes), F32),
            pltpu.VMEM(fixed.shape, F32),
            pltpu.VMEM((8, SUB), F32),
            pltpu.VMEM((n, 8, SUB), F32),
            pltpu.VMEM((n, PACKED, SUB), F32),
            pltpu.VMEM((FIELDS, SUB, count * SUB), F32),
            pltpu.VMEM(piece_shape, F32),
            pltpu.VMEM((modes, pixels), F32),
            pltpu.VMEM((MODE_ROWS, pixels), F32),
            pltpu.VMEM((2 * SUB, pixels), BF16),
            pltpu.VMEM(pack.shape, BF16),
            pltpu.VMEM((share * SUB, SUB), F32),
            pltpu.VMEM((share * SUB, SUB), F32),
            pltpu.VMEM((share, FIELDS * HALF, 2 * SUB), F32),
            pltpu.VMEM((share, SUB, 2 * FIELDS * SUB), F32),
            pltpu.VMEM((share, 2, FIELDS * BAND, SUB), F32),
            pltpu.VMEM((share, FIELDS * HALF, 2 * SUB), F32),
            pltpu.VMEM(((share + 1) * FRAMES + 4, SUB), F32),
            pltpu.VMEM((share + 1, 8, SUB), F32),
            pltpu.VMEM((ITERS, PACKED, SUB), F32),
            pltpu.VMEM((ITERS, n, PACKED, SUB), F32),
            pltpu.VMEM((8, SUB), F32),
            pltpu.SemaphoreType.DMA((6,)),
            pltpu.SemaphoreType.DMA((1 + ITERS,)),
            pltpu.SemaphoreType.DMA((1 + ITERS,)),
            pltpu.SemaphoreType.DMA((2,)),
            pltpu.SemaphoreType.DMA((count,)),
            pltpu.SemaphoreType.DMA((count,)),
            pltpu.SemaphoreType.DMA((1,)),
            pltpu.SemaphoreType.DMA((1,)),
        ],
        compiler_params=pltpu.CompilerParams(
            collective_id=0, has_side_effects=True, vmem_limit_bytes=VMEM_LIMIT
        ),
    )(
        images.reshape(FIELDS, rows, width),
        anchors,
        patches,
        coeffs.transpose(0, 2, 1),
        zbasis,
        fixed,
        pack,
    )
    both = both.transpose(0, 2, 1)
    return both[:FRAMES], both[FRAMES:]


def solution(mesh):
    return jax.shard_map(
        on_device,
        mesh=mesh,
        in_specs=(P(None, None, "sub", None), P("sub"), P("sub"), P(None, None, "sub"), P()),
        out_specs=(P(None, None, "sub"), P(None, None, "sub")),
        check_vma=False,
    )
```
